256 devices in a mesh: outer: 8 (over y_hi, x), inner: 32 (over z, y_lo, core).
Axes of the slice: x: 4, y: 4 (y_hi: 2, y_lo: 2; y = y_hi * 2 + y_lo), z: 8, core: 2. Of those that a mesh axis runs over, the one named last changes fastest.
Arguments:
- weights: float32 [131072, 128], P(('outer', 'inner')), may hold values from -0.375 to 0.375
Outputs:
- level_weights: float32 [131072, 128], P(('outer', 'inner'))
The draws below stay inside these ranges and needn't reach their ends.
All inputs are finite; a program needn't handle non-finite values.
Results may differ from the reference program's by a relative error of at most 0.0049.
Values sent between devices are 32-bit elements; how exact they have to be, the bound alone decides.
A program may use at most 64 MiB of HBM per device.

```python
import jax
import jax.numpy as jnp
import numpy as np
from jax import lax

GRID_N = 16384
TREE_LEVELS = 11
PAIRS_DEV = 512
PAIRS = 131072
LEVELS = 8
N_OUTER = 8
N_INNER = 32


def level_of(rng, extent, cuts, smallest, high):
    gain = 1.0
    for dim, blocks in cuts:
        draws = jax.random.uniform(jax.random.fold_in(jax.random.fold_in(rng, 6), dim), (blocks,), jnp.float32, smallest / len(cuts), high / len(cuts))
        gain = gain * jnp.repeat(jnp.exp(draws), extent[dim] // blocks).reshape((-1,) + (1,) * (len(extent) - 1 - dim))
    return gain


def centred(stream_key, dims, spread, bound, split=(), kind=jnp.bfloat16):
    loudness = level_of(stream_key, dims, split, -0.22, 0.18) if split else 1.0
    result = jax.random.normal(stream_key, dims, jnp.float32) * spread * loudness
    return jnp.minimum(jnp.maximum(result, -bound), bound).astype(kind)


def setup_inputs(seed: int = 0) -> dict:
    streams_of = jax.random.split(jax.random.key(seed), 2)
    weights = centred(streams_of[0], (PAIRS, 128), (0.5 ** (LEVELS // 2)), 0.375, ((0, 256),), jnp.float32)
    return dict(weights=weights)


def chebyshev_nodes():
    return 0.5 * np.cos(np.pi * (2.0 * np.arange(8) + 1.0) / 16.0)

def lagrange_weights(which_child):
    node_values = chebyshev_nodes()
    targets = (node_values + which_child - 0.5) / 2.0
    weights_table = np.ones((8, 8))
    for anchor in range(8):
        for other_node in range(8):
            if other_node != anchor:
                weights_table[anchor, :] = weights_table[anchor, :] * (targets - node_values[other_node]) / (node_values[anchor] - node_values[other_node])
    return weights_table

def merge_matrix(dimension):
    merge_table = np.zeros((256, 128))
    for which_child in range(2):
        weights_table = lagrange_weights(which_child)
        if dimension == 0:
            block_table = np.kron(weights_table, np.eye(8))
        else:
            block_table = np.kron(np.eye(8), weights_table)
        for component in range(2):
            merge_table[which_child * 128 + component * 64:which_child * 128 + component * 64 + 64, component * 64:component * 64 + 64] = block_table.T
    return jnp.asarray(merge_table, dtype=jnp.float32)

def level_plan(local_bits, inner_bits, outer_bits):
    levels_total = inner_bits + outer_bits
    source_bits = [[], []]
    for level_number in range(levels_total):
        source_bits[(level_number + 1) % 2].append(local_bits + level_number)
    source_bits[0] = source_bits[0] + [local_bits - 7, local_bits - 6, local_bits - 5]
    source_bits[1] = source_bits[1] + [local_bits - 4, local_bits - 3, local_bits - 2, local_bits - 1]
    target_bits = [[], []]
    for ordinal in range(local_bits - 7):
        target_bits[ordinal % 2].append(ordinal)
    level_list = []
    for level_number in range(levels_total):
        dimension = (level_number + 1) % 2
        carried_bit = local_bits + level_number
        if level_number < inner_bits:
            moved_bit = local_bits - inner_bits + level_number
        else:
            moved_bit = local_bits - levels_total + level_number - inner_bits
        level_list.append((dimension, carried_bit, moved_bit, [list(bit_group) for bit_group in target_bits], [list(bit_group) for bit_group in source_bits]))
        target_bits = [[carried_bit if bit_place == moved_bit else bit_place for bit_place in bit_group] for bit_group in target_bits]
        source_bits = [[carried_bit if bit_place == moved_bit else bit_place for bit_place in bit_group] for bit_group in source_bits]
        source_bits[dimension] = source_bits[dimension][1:]
        target_bits[dimension] = [moved_bit] + target_bits[dimension]
    return level_list

def bit_value(row_index, positions):
    assembled = jnp.zeros_like(row_index)
    for ordinal, position in enumerate(positions):
        assembled = assembled + ((row_index >> position & 1) << ordinal)
    return assembled

def spread_grid(values, axis_place):
    row_count = values.shape[0]
    if axis_place == 0:
        shaped = values[:, None, :, None]
    else:
        shaped = values[:, None, None, :]
    return jnp.broadcast_to(shaped, (row_count, 2, 8, 8)).reshape(row_count, 128)

def dimension_terms(target_index, target_level, source_index, source_level):
    node_values = jnp.asarray(chebyshev_nodes(), dtype=jnp.float32)
    box_width = 2.0 ** (-source_level)
    center = (target_index.astype(jnp.float32) + 0.5) * (GRID_N * 2.0 ** (-target_level)) - GRID_N / 2.0
    offsets = node_values * box_width
    position = (source_index.astype(jnp.float32) + 0.5)[:, None] * box_width + offsets[None, :]
    linear = offsets[None, :] * center[:, None]
    return (center, position, linear)

def phase_cycles(target_index, target_level, source_index, source_level):
    center_one, place_one, linear_one = dimension_terms(target_index[0], target_level[0], source_index[0], source_level[0])
    center_two, place_two, linear_two = dimension_terms(target_index[1], target_level[1], source_index[1], source_level[1])
    turn = 2.0 * np.pi
    sine_one = spread_grid(jnp.sin(turn * place_one), 0)
    sine_two = spread_grid(jnp.sin(turn * place_two), 1)
    cosine_one = spread_grid(jnp.cos(turn * place_one), 0)
    cosine_two = spread_grid(jnp.cos(turn * place_two), 1)
    coeff_one = (2.0 + sine_one * sine_two) / 16.0
    coeff_two = (2.0 + cosine_one * cosine_two) / 16.0
    radial = jnp.sqrt((coeff_one * center_one[:, None]) ** 2 + (coeff_two * center_two[:, None]) ** 2)
    linear = spread_grid(linear_one, 0) + spread_grid(linear_two, 1)
    return linear - jnp.floor(linear) + (radial - jnp.floor(radial))

def rotate(values, cycles, direction):
    radians = 2.0 * np.pi * cycles
    cosine = jnp.cos(radians)
    sine_part = jnp.sin(radians) * direction
    swapped = jnp.concatenate([values[:, 64:], values[:, :64]], axis=1)
    sign_pattern = jnp.concatenate([-jnp.ones((64,), jnp.float32), jnp.ones((64,), jnp.float32)])
    return values * cosine + swapped * (sine_part * sign_pattern)

def combine(first_child, second_child, base_index, layout, merge_table):
    dimension, target_bits, source_bits = (layout[0], layout[3], layout[4])
    children = [first_child, second_child]
    target_index = [bit_value(base_index, target_bits[0]), bit_value(base_index, target_bits[1])]
    source_index = [bit_value(base_index, source_bits[0]), bit_value(base_index, source_bits[1])]
    source_level = [len(source_bits[0]), len(source_bits[1])]
    target_level = [TREE_LEVELS - source_level[0], TREE_LEVELS - source_level[1]]
    results = []
    for branch in range(2):
        new_target = list(target_index)
        new_target[dimension] = 2 * target_index[dimension] + branch
        new_level = list(target_level)
        new_level[dimension] = target_level[dimension] + 1
        rotated = []
        for which_child in range(2):
            child_source = list(source_index)
            child_source[dimension] = source_index[dimension] + which_child
            rotated.append(rotate(children[which_child], phase_cycles(new_target, new_level, child_source, source_level), 1.0))
        stacked = jnp.concatenate(rotated, axis=1)
        merged = jnp.dot(stacked, merge_table, precision=lax.Precision.HIGHEST, preferred_element_type=jnp.float32)
        parent_source = list(source_index)
        parent_source[dimension] = source_index[dimension] // 2
        parent_level = list(source_level)
        parent_level[dimension] = source_level[dimension] - 1
        results.append(rotate(merged, phase_cycles(new_target, new_level, parent_source, parent_level), -1.0))
    return results

def reference(weights):
    local_bits = PAIRS_DEV.bit_length() - 1
    inner_bits = N_INNER.bit_length() - 1
    outer_bits = N_OUTER.bit_length() - 1
    row_count = weights.shape[0]
    current = weights
    for layout in level_plan(local_bits, inner_bits, outer_bits):
        dimension, carried_bit, moved_bit = (layout[0], layout[1], layout[2])
        merge_table = merge_matrix(dimension)
        outer_count = row_count >> carried_bit + 1
        middle_count = 2 ** (carried_bit - moved_bit - 1)
        inner_count = 2 ** moved_bit
        shaped = current.reshape(outer_count, 2, middle_count, 2, inner_count, 128)
        indices = jnp.arange(row_count, dtype=jnp.int32).reshape(outer_count, 2, middle_count, 2, inner_count)[:, 0].reshape(-1)
        first_child = shaped[:, 0].reshape(-1, 128)
        second_child = shaped[:, 1].reshape(-1, 128)
        outputs = combine(first_child, second_child, indices, layout, merge_table)
        stacked = jnp.stack([branch_out.reshape(outer_count, middle_count, 2, inner_count, 128) for branch_out in outputs], axis=3)
        current = jnp.moveaxis(stacked, 2, 1).reshape(row_count, 128)
    return current
```

```python
import functools

import jax
import jax.numpy as jnp
import numpy as np
from jax import lax
from jax.experimental import pallas as pl
from jax.experimental.pallas import tpu as pltpu
from jax.sharding import PartitionSpec as P

MESH = pl.DeviceIdType.MESH
F32 = jnp.float32
BF16 = jnp.bfloat16
GRID_N = 16384.0
LEVELS = 8
TILES = 32


def chebyshev_nodes():
    return 0.5 * np.cos(np.pi * (2.0 * np.arange(8) + 1.0) / 16.0)


def lagrange_weights(which_child):
    node = chebyshev_nodes()
    targets = (node + which_child - 0.5) / 2.0
    table = np.ones((8, 8))
    for anchor in range(8):
        for other in range(8):
            if other != anchor:
                table[anchor] *= (targets - node[other]) / (node[anchor] - node[other])
    return table


def merge_matrix(dimension):
    parts = []
    for child in range(2):
        table = lagrange_weights(child)
        full = np.kron(table, np.eye(8)) if dimension == 0 else np.kron(np.eye(8), table)
        parts.append(full.T)
    one = np.concatenate(parts, axis=0)
    out = np.zeros((256, 128))
    out[:128, :64] = one
    out[128:, 64:] = one
    return out


def even_fit(values, terms):
    z = 0.125 * (1.0 - np.cos(np.pi * (np.arange(400) + 0.5) / 400))
    basis = np.polynomial.chebyshev.Chebyshev.fit(z, values(np.sqrt(z)), terms - 1, domain=[0, 0.25])
    return [float(c) for c in basis.convert(kind=np.polynomial.Polynomial).coef]


SIN_COEF = even_fit(lambda f: np.sin(2 * np.pi * f) / f, 6)
COS_COEF = even_fit(lambda f: np.cos(2 * np.pi * f), 7)


def horner(coef, z):
    total = jnp.full_like(z, coef[-1])
    for c in coef[-2::-1]:
        total = total * z + c
    return total


def nearest(v):
    return jnp.floor(v + 0.5)


def turn(cycles):
    f = cycles - nearest(cycles)
    z = f * f
    return horner(COS_COEF, z), f * horner(SIN_COEF, z)


def widths(level):
    odd = len([m for m in range(level) if m % 2 == 1])
    even = len([m for m in range(level) if m % 2 == 0])
    h = (2.0 ** -(3 + 4 - odd), 2.0 ** -(4 + 4 - even))
    w = (GRID_N * 2.0 ** -(4 + odd), GRID_N * 2.0 ** -(3 + even))
    return h, w


def place_terms(level):
    terms = []
    for m in range(level, LEVELS):
        e = (m + 1) % 2
        weight = 2.0 ** -(7 - (m - 1) // 2) if e == 0 else 2.0 ** -(8 - m // 2)
        if m == level:
            where = ("lane", 6)
        elif m <= 5:
            where = ("lead", m - 1)
        else:
            where = ("sub", m - 5)
        terms.append((*where, e, weight))
    return terms


def frequency_terms(level):
    terms = [("sub", 0, 0, 1024.0)]
    for m in range(level):
        e = (m + 1) % 2
        weight = 512.0 / 2 ** (m // 2) if e == 0 else 1024.0 / 2 ** (m // 2)
        if m <= 4:
            where = ("lead", m)
        elif m <= 6:
            where = ("sub", m - 4)
        else:
            where = ("lane", 6)
        terms.append((*where, e, weight))
    return terms


def vector_part(terms, e, sub, lane, base):
    total = jnp.full((8, 128), base, F32)
    for where, bit, dim, weight in terms:
        if dim == e and where != "lead":
            source = sub if where == "sub" else lane
            total = total + ((source >> bit) & 1).astype(F32) * weight
    return total


def lead_part(terms, e, index, scale):
    total = jnp.int32(0)
    for where, bit, dim, weight in terms:
        if dim == e and where == "lead":
            total = total + ((index >> bit) & 1) * int(weight * scale)
    return total


def grid_offset(level):
    return sum(max(TILES >> l, 1) for l in range(level))


GRID_TILES = grid_offset(LEVELS + 1)


def device_bits(dest):
    d1 = ((dest >> 6) & 1) + 2 * ((dest >> 7) & 1) + 4 * (dest & 1)
    d2 = (dest >> 1) & 15
    d5 = (dest >> 5) & 1
    return d1, d2, d5


def coefficient_tiles(me, tau_ref, g_ref, sub, lane):
    d1, d2, _ = device_bits(me)
    tau = (tau_ref[0:1, :], tau_ref[1:2, :])
    for level in range(LEVELS + 1):
        h, _ = widths(level)
        terms = place_terms(level)
        base = [vector_part(terms, e, sub, lane, 0.5 * h[e]) + h[e] * tau[e] for e in range(2)]
        count = max(TILES >> level, 1)

        def tile(u, carry, level=level, base=base, terms=terms):
            index = u << level
            x1 = base[0] + (d1 * 32 + lead_part(terms, 0, index, 256)).astype(F32) * (1 / 256)
            x2 = base[1] + (d2 * 16 + lead_part(terms, 1, index, 256)).astype(F32) * (1 / 256)
            cos1, sin1 = turn(x1)
            cos2, sin2 = turn(x2)
            g1 = (2.0 + sin1 * sin2) * (1 / 16)
            g2 = (2.0 + cos1 * cos2) * (1 / 16)
            g_ref[0, grid_offset(level) + u] = g1 * g1
            g_ref[1, grid_offset(level) + u] = g2 * g2
            return carry

        lax.fori_loop(0, count, tile, 0, unroll=min(count, 2))


def factor_tiles(me, level, tau_ref, g_ref, cos_ref, sin_ref, sub, lane):
    _, _, d5 = device_bits(me)
    tau = (tau_ref[0:1, :], tau_ref[1:2, :])
    h, w = widths(level)
    e = (level + 1) % 2
    terms = frequency_terms(level)
    base = [vector_part(terms, d, sub, lane, 0.5 * w[d] - GRID_N / 2) for d in range(2)]
    slope = [h[d] * tau[d] for d in range(2)]

    def whole(k1, k2, g1, g2):
        lin = slope[0] * k1 + slope[1] * k2
        rad = jnp.sqrt(g1 * (k1 * k1) + g2 * (k2 * k2))
        return (lin - nearest(lin)) + (rad - nearest(rad))

    def tile(i, carry):
        k1 = base[0] + lead_part(terms, 0, i, 1).astype(F32)
        k2 = base[1] + (d5 * 2048 + lead_part(terms, 1, i, 1)).astype(F32)
        u = grid_offset(level) + (i >> min(level, 5))
        g1, g2 = g_ref[0, u], g_ref[1, u]
        if level == LEVELS:
            cos_ref[2 * level, i], sin_ref[2 * level, i] = turn(whole(k1, k2, g1, g2))
            return carry
        if level > 0:
            square = g1 * (k1 * k1) + g2 * (k2 * k2)
            rad = jnp.sqrt(square)
        for j in range(2):
            step = (2 * j - 1) * w[e] / 4
            if level == 0:
                cycles = whole(k1, k2 + step, g1, g2)
            else:
                k, g = (k1, g1) if e == 0 else (k2, g2)
                extra = g * (step * (2.0 * k + step))
                cycles = slope[e] * step + extra / (jnp.sqrt(square + extra) + rad)
            cos_ref[2 * level + j, i], sin_ref[2 * level + j, i] = turn(cycles)
        return carry

    lax.fori_loop(0, TILES, tile, 0, unroll=2)


def split(value):
    high = value.astype(BF16)
    low = (value - high.astype(F32)).astype(BF16)
    return high, low


def merge(left, right, w_high, w_low):
    n = left.shape[0]
    lh, ll = split(left)
    rh, rl = split(right)
    high = jnp.concatenate([lh.reshape(8 * n, 128), rh.reshape(8 * n, 128)], axis=1)
    low = jnp.concatenate([ll.reshape(8 * n, 128), rl.reshape(8 * n, 128)], axis=1)
    total = jnp.dot(high, w_high, preferred_element_type=F32)
    total += jnp.dot(low, w_high, preferred_element_type=F32)
    total += jnp.dot(high, w_low, preferred_element_type=F32)
    return total.reshape(n, 8, 128)


def run_levels(recv, out_ref, cos_ref, sin_ref, w_refs, state, sub, lane):
    low_lane = lane < 64
    first, second = recv[0], recv[1]
    first_t, second_t = pltpu.roll(first, 64, 2), pltpu.roll(second, 64, 2)
    state[0] = jnp.where(low_lane[None], first, second_t)
    state[1] = jnp.where(low_lane[None], first_t, second)
    for level in range(LEVELS):
        e = (level + 1) % 2
        w_high, w_low = w_refs[2 * e][...], w_refs[2 * e + 1][...]
        re, im = state[0], state[1]
        turned = []
        for j in range(2):
            c, s = cos_ref[2 * level + j], sin_ref[2 * level + j]
            turned.append((re * c - im * s, im * c + re * s))
        for part in range(2):
            r0, r1 = turned[0][part], turned[1][part]
            if level < 5:
                lo = 1 << level
                hi = TILES // (2 * lo)
                outs = []
                for r in (r0, r1):
                    v = r.reshape(hi, 2, lo, 8, 128)
                    left = v[:, 0].reshape(16, 8, 128)
                    right = v[:, 1].reshape(16, 8, 128)
                    outs.append(merge(left, right, w_high, w_low).reshape(hi, 1, lo, 8, 128))
                new = jnp.concatenate(outs, axis=1).reshape(TILES, 8, 128)
            elif level < 7:
                bit = level - 4
                keep = (((sub >> bit) & 1) == 0)[None]
                shift = 1 << bit
                left = jnp.where(keep, r0, pltpu.roll(r1, shift, 1))
                right = jnp.where(keep, pltpu.roll(r0, 8 - shift, 1), r1)
                new = merge(left, right, w_high, w_low)
            else:
                new = merge(r0, r1, w_high, w_low)
            state[part] = new
    re, im = state[0], state[1]
    c, s = cos_ref[2 * LEVELS], sin_ref[2 * LEVELS]
    w_re, w_im = re * c + im * s, im * c - re * s
    even = jnp.where(low_lane[None], w_re, pltpu.roll(w_im, 64, 2))
    odd = jnp.where(low_lane[None], pltpu.roll(w_re, 64, 2), w_im)
    out_ref[...] = jnp.concatenate([even[:, None], odd[:, None]], axis=1)


def mesh_id(d):
    return (d >> 5, d & 31)


def kernel(x_ref, tau_ref, w0, w1, w2, w3, out_ref, recv, state, g_ref, cos_ref, sin_ref, send_sem, recv_sem, own_sem):
    me = lax.axis_index("outer") * 32 + lax.axis_index("inner")
    barrier = pltpu.get_barrier_semaphore()

    def greet(k, carry):
        pl.semaphore_signal(barrier, inc=1, device_id=mesh_id((me + k) & 255), device_id_type=MESH)
        return carry

    lax.fori_loop(1, 256, greet, 0, unroll=5)
    sub = lax.broadcasted_iota(jnp.int32, (8, 128), 0)
    lane = lax.broadcasted_iota(jnp.int32, (8, 128), 1)
    coefficient_tiles(me, tau_ref, g_ref, sub, lane)
    for level in range(LEVELS + 1):
        factor_tiles(me, level, tau_ref, g_ref, cos_ref, sin_ref, sub, lane)
    pl.semaphore_wait(barrier, 255)
    place = recv.at[me & 1, (me >> 1) & 31, me >> 6]
    own = pltpu.make_async_copy(x_ref.at[(me & 31) * 8 + (me >> 5)], place, own_sem)
    own.start()

    def send(k, carry):
        d = (me + k) & 255
        pltpu.make_async_remote_copy(
            src_ref=x_ref.at[(d & 31) * 8 + (d >> 5)],
            dst_ref=place,
            send_sem=send_sem,
            recv_sem=recv_sem,
            device_id=mesh_id(d),
            device_id_type=MESH,
        ).start()
        return carry

    lax.fori_loop(1, 256, send, 0, unroll=5)
    own.wait()
    most = x_ref.at[pl.ds(0, 255)]
    pltpu.make_async_copy(most, most, recv_sem).wait()
    pltpu.make_async_copy(most, most, send_sem).wait()
    run_levels(recv.reshape(2, TILES, 8, 128), out_ref, cos_ref, sin_ref, (w0, w1, w2, w3), state, sub, lane)


def body(weights):
    tables = []
    for dimension in range(2):
        full = jnp.asarray(merge_matrix(dimension), F32)
        high = full.astype(BF16)
        tables += [high, (full - high.astype(F32)).astype(BF16)]
    lanes = np.arange(128)
    node = chebyshev_nodes()
    tau = np.zeros((8, 128))
    tau[0], tau[1] = node[(lanes >> 3) & 7], node[lanes & 7]
    vmem = pl.BlockSpec(memory_space=pltpu.VMEM)
    out = pl.pallas_call(
        kernel,
        out_shape=jax.ShapeDtypeStruct((TILES, 2, 8, 128), F32),
        in_specs=[pl.BlockSpec(memory_space=pltpu.HBM)] + [vmem] * 5,
        out_specs=vmem,
        scratch_shapes=[
            pltpu.VMEM((2, TILES, 4, 2, 128), F32),
            pltpu.VMEM((2, TILES, 8, 128), F32),
            pltpu.VMEM((2, GRID_TILES, 8, 128), F32),
            pltpu.VMEM((2 * LEVELS + 1, TILES, 8, 128), F32),
            pltpu.VMEM((2 * LEVELS + 1, TILES, 8, 128), F32),
            pltpu.SemaphoreType.DMA,
            pltpu.SemaphoreType.DMA,
            pltpu.SemaphoreType.DMA,
        ],
        compiler_params=pltpu.CompilerParams(collective_id=0, has_side_effects=True),
    )(weights.reshape(256, 2, 128), jnp.asarray(tau, F32), *tables)
    return out.reshape(512, 128)


def solution(mesh):
    spec = P(("outer", "inner"), None)
    return jax.shard_map(body, mesh=mesh, in_specs=(spec,), out_specs=spec, check_vma=False)
```

```python
import functools

import jax
import jax.numpy as jnp
import numpy as np
from jax import lax
from jax.experimental import pallas as pl
from jax.experimental.pallas import tpu as pltpu
from jax.sharding import PartitionSpec as P

LOGICAL = pl.DeviceIdType.LOGICAL
F32 = jnp.float32
BF16 = jnp.bfloat16
GRID_N = 16384.0
LEVELS = 8
TILES = 32


def chebyshev_nodes():
    return 0.5 * np.cos(np.pi * (2.0 * np.arange(8) + 1.0) / 16.0)


def lagrange_weights(which_child):
    node = chebyshev_nodes()
    targets = (node + which_child - 0.5) / 2.0
    table = np.ones((8, 8))
    for anchor in range(8):
        for other in range(8):
            if other != anchor:
                table[anchor] *= (targets - node[other]) / (node[anchor] - node[other])
    return table


def merge_matrix(dimension):
    parts = []
    for child in range(2):
        table = lagrange_weights(child)
        full = np.kron(table, np.eye(8)) if dimension == 0 else np.kron(np.eye(8), table)
        parts.append(full.T)
    one = np.concatenate(parts, axis=0)
    out = np.zeros((256, 128))
    out[:128, :64] = one
    out[128:, 64:] = one
    return out


def even_fit(values, terms):
    z = 0.125 * (1.0 - np.cos(np.pi * (np.arange(400) + 0.5) / 400))
    basis = np.polynomial.chebyshev.Chebyshev.fit(z, values(np.sqrt(z)), terms - 1, domain=[0, 0.25])
    return [float(c) for c in basis.convert(kind=np.polynomial.Polynomial).coef]


SIN_COEF = even_fit(lambda f: np.sin(2 * np.pi * f) / f, 6)
COS_COEF = even_fit(lambda f: np.cos(2 * np.pi * f), 7)


def horner(coef, z):
    total = jnp.full_like(z, coef[-1])
    for c in coef[-2::-1]:
        total = total * z + c
    return total


def nearest(v):
    return jnp.floor(v + 0.5)


def turn(cycles):
    f = cycles - nearest(cycles)
    z = f * f
    return horner(COS_COEF, z), f * horner(SIN_COEF, z)


def widths(level):
    odd = len([m for m in range(level) if m % 2 == 1])
    even = len([m for m in range(level) if m % 2 == 0])
    h = (2.0 ** -(3 + 4 - odd), 2.0 ** -(4 + 4 - even))
    w = (GRID_N * 2.0 ** -(4 + odd), GRID_N * 2.0 ** -(3 + even))
    return h, w


def place_terms(level):
    terms = []
    for m in range(level, LEVELS):
        e = (m + 1) % 2
        weight = 2.0 ** -(7 - (m - 1) // 2) if e == 0 else 2.0 ** -(8 - m // 2)
        if m == level:
            where = ("lane", 6)
        elif m <= 5:
            where = ("lead", m - 1)
        else:
            where = ("sub", m - 5)
        terms.append((*where, e, weight))
    return terms


def frequency_terms(level):
    terms = [("sub", 0, 0, 1024.0)]
    for m in range(level):
        e = (m + 1) % 2
        weight = 512.0 / 2 ** (m // 2) if e == 0 else 1024.0 / 2 ** (m // 2)
        if m <= 4:
            where = ("lead", m)
        elif m <= 6:
            where = ("sub", m - 4)
        else:
            where = ("lane", 6)
        terms.append((*where, e, weight))
    return terms


def vector_part(terms, e, sub, lane, base):
    total = jnp.full((8, 128), base, F32)
    for where, bit, dim, weight in terms:
        if dim == e and where != "lead":
            source = sub if where == "sub" else lane
            total = total + ((source >> bit) & 1).astype(F32) * weight
    return total


def lead_part(terms, e, index, scale):
    total = jnp.int32(0)
    for where, bit, dim, weight in terms:
        if dim == e and where == "lead":
            total = total + ((index >> bit) & 1) * int(weight * scale)
    return total


def grid_offset(level):
    return sum(max(TILES >> l, 1) for l in range(level))


GRID_TILES = grid_offset(LEVELS + 1)


def device_bits(dest):
    d1 = ((dest >> 6) & 1) + 2 * ((dest >> 7) & 1) + 4 * (dest & 1)
    d2 = (dest >> 1) & 15
    d5 = (dest >> 5) & 1
    return d1, d2, d5


def coefficient_tiles(me, tau_ref, g_ref, sub, lane):
    d1, d2, _ = device_bits(me)
    tau = (tau_ref[0:1, :], tau_ref[1:2, :])
    for level in range(LEVELS + 1):
        h, _ = widths(level)
        terms = place_terms(level)
        base = [vector_part(terms, e, sub, lane, 0.5 * h[e]) + h[e] * tau[e] for e in range(2)]
        count = max(TILES >> level, 1)

        def tile(u, carry, level=level, base=base, terms=terms):
            index = u << level
            x1 = base[0] + (d1 * 32 + lead_part(terms, 0, index, 256)).astype(F32) * (1 / 256)
            x2 = base[1] + (d2 * 16 + lead_part(terms, 1, index, 256)).astype(F32) * (1 / 256)
            cos1, sin1 = turn(x1)
            cos2, sin2 = turn(x2)
            g1 = (2.0 + sin1 * sin2) * (1 / 16)
            g2 = (2.0 + cos1 * cos2) * (1 / 16)
            g_ref[0, grid_offset(level) + u] = g1 * g1
            g_ref[1, grid_offset(level) + u] = g2 * g2
            return carry

        lax.fori_loop(0, count, tile, 0, unroll=min(count, 2))


def factor_tiles(me, level, tau_ref, g_ref, cos_ref, sin_ref, sub, lane):
    _, _, d5 = device_bits(me)
    tau = (tau_ref[0:1, :], tau_ref[1:2, :])
    h, w = widths(level)
    e = (level + 1) % 2
    terms = frequency_terms(level)
    base = [vector_part(terms, d, sub, lane, 0.5 * w[d] - GRID_N / 2) for d in range(2)]
    slope = [h[d] * tau[d] for d in range(2)]

    def whole(k1, k2, g1, g2):
        lin = slope[0] * k1 + slope[1] * k2
        rad = jnp.sqrt(g1 * (k1 * k1) + g2 * (k2 * k2))
        return (lin - nearest(lin)) + (rad - nearest(rad))

    def tile(i, carry):
        k1 = base[0] + lead_part(terms, 0, i, 1).astype(F32)
        k2 = base[1] + (d5 * 2048 + lead_part(terms, 1, i, 1)).astype(F32)
        u = grid_offset(level) + (i >> min(level, 5))
        g1, g2 = g_ref[0, u], g_ref[1, u]
        if level == LEVELS:
            cos_ref[2 * level, i], sin_ref[2 * level, i] = turn(whole(k1, k2, g1, g2))
            return carry
        if level > 0:
            square = g1 * (k1 * k1) + g2 * (k2 * k2)
            rad = jnp.sqrt(square)
        for j in range(2):
            step = (2 * j - 1) * w[e] / 4
            if level == 0:
                cycles = whole(k1, k2 + step, g1, g2)
            else:
                k, g = (k1, g1) if e == 0 else (k2, g2)
                extra = g * (step * (2.0 * k + step))
                cycles = slope[e] * step + extra / (jnp.sqrt(square + extra) + rad)
            cos_ref[2 * level + j, i], sin_ref[2 * level + j, i] = turn(cycles)
        return carry

    lax.fori_loop(0, TILES, tile, 0, unroll=2)


def split(value):
    high = value.astype(BF16)
    low = (value - high.astype(F32)).astype(BF16)
    return high, low


def merge(left, right, w_high, w_low):
    n = left.shape[0]
    lh, ll = split(left)
    rh, rl = split(right)
    high = jnp.concatenate([lh.reshape(8 * n, 128), rh.reshape(8 * n, 128)], axis=1)
    low = jnp.concatenate([ll.reshape(8 * n, 128), rl.reshape(8 * n, 128)], axis=1)
    total = jnp.dot(high, w_high, preferred_element_type=F32)
    total += jnp.dot(low, w_high, preferred_element_type=F32)
    total += jnp.dot(high, w_low, preferred_element_type=F32)
    return total.reshape(n, 8, 128)


def run_levels(recv, out_ref, cos_ref, sin_ref, w_ref, state, sub, lane):
    low_lane = lane < 64
    first, second = recv[0], recv[1]
    first_t, second_t = pltpu.roll(first, 64, 2), pltpu.roll(second, 64, 2)
    state[0] = jnp.where(low_lane[None], first, second_t)
    state[1] = jnp.where(low_lane[None], first_t, second)
    for level in range(LEVELS):
        e = (level + 1) % 2
        w_high, w_low = w_ref[2 * e], w_ref[2 * e + 1]
        re, im = state[0], state[1]
        turned = []
        for j in range(2):
            c, s = cos_ref[2 * level + j], sin_ref[2 * level + j]
            turned.append((re * c - im * s, im * c + re * s))
        for part in range(2):
            r0, r1 = turned[0][part], turned[1][part]
            if level < 5:
                lo = 1 << level
                hi = TILES // (2 * lo)
                outs = []
                for r in (r0, r1):
                    v = r.reshape(hi, 2, lo, 8, 128)
                    left = v[:, 0].reshape(16, 8, 128)
                    right = v[:, 1].reshape(16, 8, 128)
                    outs.append(merge(left, right, w_high, w_low).reshape(hi, 1, lo, 8, 128))
                new = jnp.concatenate(outs, axis=1).reshape(TILES, 8, 128)
            elif level < 7:
                bit = level - 4
                keep = (((sub >> bit) & 1) == 0)[None]
                shift = 1 << bit
                left = jnp.where(keep, r0, pltpu.roll(r1, shift, 1))
                right = jnp.where(keep, pltpu.roll(r0, 8 - shift, 1), r1)
                new = merge(left, right, w_high, w_low)
            else:
                new = merge(r0, r1, w_high, w_low)
            state[part] = new
    re, im = state[0], state[1]
    c, s = cos_ref[2 * LEVELS], sin_ref[2 * LEVELS]
    w_re, w_im = re * c + im * s, im * c - re * s
    even = jnp.where(low_lane[None], w_re, pltpu.roll(w_im, 64, 2))
    odd = jnp.where(low_lane[None], pltpu.roll(w_re, 64, 2), w_im)
    out_ref[...] = jnp.concatenate([even[:, None], odd[:, None]], axis=1)


FAR = 0xD0


def farthest_first(n):
    return n ^ FAR


def over_others(action):
    def step(n, carry):
        action(farthest_first(n))
        return carry

    lax.fori_loop(0, FAR, step, 0, unroll=8)
    lax.fori_loop(FAR + 1, 256, step, 0, unroll=47)


def kernel(x_ref, tau_hbm, w_hbm, out_ref, recv, state, g_ref, cos_ref, sin_ref, tau_ref, w_ref, send_sem, recv_sem, own_sem, table_sem):
    me = lax.axis_index("outer") * 32 + lax.axis_index("inner")
    barrier = pltpu.get_barrier_semaphore()
    over_others(lambda k: pl.semaphore_signal(barrier, inc=1, device_id=me ^ k, device_id_type=LOGICAL))
    place = recv.at[me & 1, (me >> 1) & 31, me >> 6]
    copies = [
        pltpu.make_async_copy(tau_hbm, tau_ref, table_sem.at[0]),
        pltpu.make_async_copy(w_hbm, w_ref, table_sem.at[1]),
        pltpu.make_async_copy(x_ref.at[(me & 31) * 8 + (me >> 5)], place, own_sem),
    ]
    for copy in copies:
        copy.start()
    sub = lax.broadcasted_iota(jnp.int32, (8, 128), 0)
    lane = lax.broadcasted_iota(jnp.int32, (8, 128), 1)
    pl.semaphore_wait(barrier, 255)

    def send(k):
        d = me ^ k
        pltpu.make_async_remote_copy(
            src_ref=x_ref.at[(d & 31) * 8 + (d >> 5)],
            dst_ref=place,
            send_sem=send_sem,
            recv_sem=recv_sem,
            device_id=d,
            device_id_type=LOGICAL,
        ).start()

    over_others(send)
    for copy in copies:
        copy.wait()
    coefficient_tiles(me, tau_ref, g_ref, sub, lane)
    for level in range(LEVELS + 1):
        factor_tiles(me, level, tau_ref, g_ref, cos_ref, sin_ref, sub, lane)
    most = x_ref.at[pl.ds(0, 255)]
    pltpu.make_async_copy(most, most, recv_sem).wait()
    pltpu.make_async_copy(most, most, send_sem).wait()
    run_levels(recv.reshape(2, TILES, 8, 128), out_ref, cos_ref, sin_ref, w_ref, state, sub, lane)


def body(weights):
    tables = []
    for dimension in range(2):
        full = jnp.asarray(merge_matrix(dimension), F32)
        high = full.astype(BF16)
        tables += [high, (full - high.astype(F32)).astype(BF16)]
    lanes = np.arange(128)
    node = chebyshev_nodes()
    tau = np.zeros((8, 128))
    tau[0], tau[1] = node[(lanes >> 3) & 7], node[lanes & 7]
    vmem = pl.BlockSpec(memory_space=pltpu.VMEM)
    out = pl.pallas_call(
        kernel,
        out_shape=pltpu.VMEM((TILES, 2, 8, 128), F32),
        in_specs=[pl.BlockSpec(memory_space=pltpu.HBM)] * 3,
        out_specs=vmem,
        scratch_shapes=[
            pltpu.VMEM((2, TILES, 4, 2, 128), F32),
            pltpu.VMEM((2, TILES, 8, 128), F32),
            pltpu.VMEM((2, GRID_TILES, 8, 128), F32),
            pltpu.VMEM((2 * LEVELS + 1, TILES, 8, 128), F32),
            pltpu.VMEM((2 * LEVELS + 1, TILES, 8, 128), F32),
            pltpu.VMEM((8, 128), F32),
            pltpu.VMEM((4, 256, 128), BF16),
            pltpu.SemaphoreType.DMA,
            pltpu.SemaphoreType.DMA,
            pltpu.SemaphoreType.DMA,
            pltpu.SemaphoreType.DMA((2,)),
        ],
        compiler_params=pltpu.CompilerParams(collective_id=0, has_side_effects=True),
    )(weights.reshape(256, 2, 128), jnp.asarray(tau, F32), jnp.stack(tables))
    return out.reshape(512, 128)


def solution(mesh):
    spec = P(("outer", "inner"), None)
    return jax.shard_map(body, mesh=mesh, in_specs=(spec,), out_specs=spec, check_vma=False)
```

```python
import functools

import jax
import jax.numpy as jnp
import numpy as np
from jax import lax
from jax.experimental import pallas as pl
from jax.experimental.pallas import tpu as pltpu
from jax.sharding import PartitionSpec as P

LOGICAL = pl.DeviceIdType.LOGICAL
F32 = jnp.float32
BF16 = jnp.bfloat16
GRID_N = 16384.0
LEVELS = 8
TILES = 32
EARLY_PLANES = 2
EXACT = (0, 1, 2, 3, 4, 5, 6, 7)


def chebyshev_nodes():
    return 0.5 * np.cos(np.pi * (2.0 * np.arange(8) + 1.0) / 16.0)


def lagrange_weights(which_child):
    node = chebyshev_nodes()
    targets = (node + which_child - 0.5) / 2.0
    table = np.ones((8, 8))
    for anchor in range(8):
        for other in range(8):
            if other != anchor:
                table[anchor] *= (targets - node[other]) / (node[anchor] - node[other])
    return table


def merge_matrix(dimension):
    parts = []
    for child in range(2):
        table = lagrange_weights(child)
        full = np.kron(table, np.eye(8)) if dimension == 0 else np.kron(np.eye(8), table)
        parts.append(full.T)
    one = np.concatenate(parts, axis=0)
    out = np.zeros((256, 128))
    out[:128, :64] = one
    out[128:, 64:] = one
    return out


def even_fit(values, terms):
    z = 0.125 * (1.0 - np.cos(np.pi * (np.arange(400) + 0.5) / 400))
    basis = np.polynomial.chebyshev.Chebyshev.fit(z, values(np.sqrt(z)), terms - 1, domain=[0, 0.25])
    return [float(c) for c in basis.convert(kind=np.polynomial.Polynomial).coef]


SIN_COEF = even_fit(lambda f: np.sin(2 * np.pi * f) / f, 6)
COS_COEF = even_fit(lambda f: np.cos(2 * np.pi * f), 7)


def horner(coef, z):
    total = jnp.full_like(z, coef[-1])
    for c in coef[-2::-1]:
        total = total * z + c
    return total


def nearest(v):
    return jnp.floor(v + 0.5)


def turn(cycles):
    f = cycles - nearest(cycles)
    z = f * f
    return horner(COS_COEF, z), f * horner(SIN_COEF, z)


def widths(level):
    odd = len([m for m in range(level) if m % 2 == 1])
    even = len([m for m in range(level) if m % 2 == 0])
    h = (2.0 ** -(3 + 4 - odd), 2.0 ** -(4 + 4 - even))
    w = (GRID_N * 2.0 ** -(4 + odd), GRID_N * 2.0 ** -(3 + even))
    return h, w


def place_terms(level):
    terms = []
    for m in range(level, LEVELS):
        e = (m + 1) % 2
        weight = 2.0 ** -(7 - (m - 1) // 2) if e == 0 else 2.0 ** -(8 - m // 2)
        if m == level:
            where = ("lane", 6)
        elif m <= 5:
            where = ("lead", m - 1)
        else:
            where = ("sub", m - 5)
        terms.append((*where, e, weight))
    return terms


def frequency_terms(level):
    terms = [("sub", 0, 0, 1024.0)]
    for m in range(level):
        e = (m + 1) % 2
        weight = 512.0 / 2 ** (m // 2) if e == 0 else 1024.0 / 2 ** (m // 2)
        if m <= 4:
            where = ("lead", m)
        elif m <= 6:
            where = ("sub", m - 4)
        else:
            where = ("lane", 6)
        terms.append((*where, e, weight))
    return terms


def vector_part(terms, e, sub, lane, base):
    total = jnp.full((8, 128), base, F32)
    for where, bit, dim, weight in terms:
        if dim == e and where != "lead":
            source = sub if where == "sub" else lane
            total = total + ((source >> bit) & 1).astype(F32) * weight
    return total


def lead_part(terms, e, index, scale):
    total = jnp.int32(0)
    for where, bit, dim, weight in terms:
        if dim == e and where == "lead":
            total = total + ((index >> bit) & 1) * int(weight * scale)
    return total


def grid_offset(level):
    return sum(max(TILES >> l, 1) for l in range(level))


GRID_TILES = grid_offset(LEVELS + 1)


def device_bits(dest):
    d1 = ((dest >> 6) & 1) + 2 * ((dest >> 7) & 1) + 4 * (dest & 1)
    d2 = (dest >> 1) & 15
    d5 = (dest >> 5) & 1
    return d1, d2, d5


def coefficient_tiles(me, tau_ref, g_ref, sub, lane):
    d1, d2, _ = device_bits(me)
    tau = (tau_ref[0:1, :], tau_ref[1:2, :])
    for level in range(LEVELS + 1):
        h, _ = widths(level)
        terms = place_terms(level)
        base = [vector_part(terms, e, sub, lane, 0.5 * h[e]) + h[e] * tau[e] for e in range(2)]
        count = max(TILES >> level, 1)

        def tile(u, carry, level=level, base=base, terms=terms):
            index = u << level
            x1 = base[0] + (d1 * 32 + lead_part(terms, 0, index, 256)).astype(F32) * (1 / 256)
            x2 = base[1] + (d2 * 16 + lead_part(terms, 1, index, 256)).astype(F32) * (1 / 256)
            cos1, sin1 = turn(x1)
            cos2, sin2 = turn(x2)
            g1 = (2.0 + sin1 * sin2) * (1 / 16)
            g2 = (2.0 + cos1 * cos2) * (1 / 16)
            g_ref[0, grid_offset(level) + u] = g1 * g1
            g_ref[1, grid_offset(level) + u] = g2 * g2
            return carry

        lax.fori_loop(0, count, tile, 0, unroll=min(count, 8))


def factor_tiles(me, level, tau_ref, g_ref, cos_ref, sin_ref, sub, lane):
    _, _, d5 = device_bits(me)
    tau = (tau_ref[0:1, :], tau_ref[1:2, :])
    h, w = widths(level)
    e = (level + 1) % 2
    terms = frequency_terms(level)
    base = [vector_part(terms, d, sub, lane, 0.5 * w[d] - GRID_N / 2) for d in range(2)]
    slope = [h[d] * tau[d] for d in range(2)]

    def whole(k1, k2, g1, g2):
        lin = slope[0] * k1 + slope[1] * k2
        rad = jnp.sqrt(g1 * (k1 * k1) + g2 * (k2 * k2))
        return (lin - nearest(lin)) + (rad - nearest(rad))

    def tile(i, carry):
        k1 = base[0] + lead_part(terms, 0, i, 1).astype(F32)
        k2 = base[1] + (d5 * 2048 + lead_part(terms, 1, i, 1)).astype(F32)
        u = grid_offset(level) + (i >> min(level, 5))
        g1, g2 = g_ref[0, u], g_ref[1, u]
        if level == LEVELS:
            cos_ref[2 * level, i], sin_ref[2 * level, i] = turn(whole(k1, k2, g1, g2))
            return carry
        if level > 0:
            square = g1 * (k1 * k1) + g2 * (k2 * k2)
            rad = jnp.sqrt(square)
        for j in range(2):
            step = (2 * j - 1) * w[e] / 4
            if level == 0:
                cycles = whole(k1, k2 + step, g1, g2)
            else:
                k, g = (k1, g1) if e == 0 else (k2, g2)
                extra = g * (step * (2.0 * k + step))
                cycles = slope[e] * step + extra / (jnp.sqrt(square + extra) + rad)
            cos_ref[2 * level + j, i], sin_ref[2 * level + j, i] = turn(cycles)
        return carry

    lax.fori_loop(0, TILES, tile, 0, unroll=8)


def merge(left, right, w_ref, dimension, exact):
    n = left.shape[0]
    values = [left.reshape(8 * n, 128), right.reshape(8 * n, 128)]
    parts = [v.astype(BF16) for v in values]
    if exact:
        parts += [(v - p.astype(F32)).astype(BF16) for v, p in zip(values, parts)]
    table = w_ref[dimension, : 128 * len(parts)]
    total = jnp.dot(jnp.concatenate(parts, axis=1), table, preferred_element_type=F32)
    return (total[:, :128] + total[:, 128:]).reshape(n, 8, 128)


def load(recv, state, lane):
    low_lane = (lane < 64)[None]
    first, second = recv[0], recv[1]
    state[0] = jnp.where(low_lane, first, pltpu.roll(second, 64, 2))
    state[1] = jnp.where(low_lane, pltpu.roll(first, 64, 2), second)


def run_levels(out_ref, cos_ref, sin_ref, w_ref, state, sub, lane):
    low_lane = lane < 64
    for level in range(LEVELS):
        e = (level + 1) % 2
        exact = level in EXACT
        re, im = state[0], state[1]
        turned = []
        for j in range(2):
            c, s = cos_ref[2 * level + j], sin_ref[2 * level + j]
            turned.append((re * c - im * s, im * c + re * s))
        for part in range(2):
            r0, r1 = turned[0][part], turned[1][part]
            if level < 5:
                lo = 1 << level
                hi = TILES // (2 * lo)
                outs = []
                for r in (r0, r1):
                    v = r.reshape(hi, 2, lo, 8, 128)
                    left = v[:, 0].reshape(16, 8, 128)
                    right = v[:, 1].reshape(16, 8, 128)
                    outs.append(merge(left, right, w_ref, e, exact).reshape(hi, 1, lo, 8, 128))
                new = jnp.concatenate(outs, axis=1).reshape(TILES, 8, 128)
            elif level < 7:
                bit = level - 4
                keep = (((sub >> bit) & 1) == 0)[None]
                shift = 1 << bit
                left = jnp.where(keep, r0, pltpu.roll(r1, shift, 1))
                right = jnp.where(keep, pltpu.roll(r0, 8 - shift, 1), r1)
                new = merge(left, right, w_ref, e, exact)
            else:
                new = merge(r0, r1, w_ref, e, exact)
            state[part] = new
    re, im = state[0], state[1]
    c, s = cos_ref[2 * LEVELS], sin_ref[2 * LEVELS]
    w_re, w_im = re * c + im * s, im * c - re * s
    even = jnp.where(low_lane[None], w_re, pltpu.roll(w_im, 64, 2))
    odd = jnp.where(low_lane[None], pltpu.roll(w_re, 64, 2), w_im)
    out_ref[...] = jnp.concatenate([even[:, None], odd[:, None]], axis=1)


FAR = 0xD0


def farthest_first(n):
    return n ^ FAR


def over_others(action):
    def step(n, carry):
        action(farthest_first(n))
        return carry

    lax.fori_loop(0, FAR, step, 0, unroll=8)
    lax.fori_loop(FAR + 1, 256, step, 0, unroll=47)


def kernel(x_ref, tau_hbm, w_hbm, out_ref, recv, state, g_ref, cos_ref, sin_ref, tau_ref, w_ref, send_sem, recv_sem, own_sem, table_sem):
    me = lax.axis_index("outer") * 32 + lax.axis_index("inner")
    barrier = pltpu.get_barrier_semaphore()
    over_others(lambda k: pl.semaphore_signal(barrier, inc=1, device_id=me ^ k, device_id_type=LOGICAL))
    place = recv.at[me & 1, (me >> 1) & 31, me >> 6]
    copies = [
        pltpu.make_async_copy(tau_hbm, tau_ref, table_sem.at[0]),
        pltpu.make_async_copy(w_hbm, w_ref, table_sem.at[1]),
        pltpu.make_async_copy(x_ref.at[(me & 31) * 8 + (me >> 5)], place, own_sem),
    ]
    for copy in copies:
        copy.start()
    sub = lax.broadcasted_iota(jnp.int32, (8, 128), 0)
    lane = lax.broadcasted_iota(jnp.int32, (8, 128), 1)
    copies[0].wait()
    early = ((me >> 2) & 7) < EARLY_PLANES

    def factors():
        coefficient_tiles(me, tau_ref, g_ref, sub, lane)
        for level in range(LEVELS + 1):
            factor_tiles(me, level, tau_ref, g_ref, cos_ref, sin_ref, sub, lane)

    @pl.when(early)
    def _():
        factors()

    pl.semaphore_wait(barrier, 255)

    def send(k):
        d = me ^ k
        pltpu.make_async_remote_copy(
            src_ref=x_ref.at[(d & 31) * 8 + (d >> 5)],
            dst_ref=place,
            send_sem=send_sem,
            recv_sem=recv_sem,
            device_id=d,
            device_id_type=LOGICAL,
        ).start()

    over_others(send)
    for copy in copies[1:]:
        copy.wait()

    @pl.when(jnp.logical_not(early))
    def _():
        factors()

    most = x_ref.at[pl.ds(0, 255)]

    pltpu.make_async_copy(most, most, recv_sem).wait()
    load(recv.reshape(2, TILES, 8, 128), state, lane)
    run_levels(out_ref, cos_ref, sin_ref, w_ref, state, sub, lane)
    pltpu.make_async_copy(most, most, send_sem).wait()


def body(weights):
    tables = []
    for dimension in range(2):
        full = jnp.asarray(merge_matrix(dimension), F32)
        high = full.astype(BF16)
        low = (full - high.astype(F32)).astype(BF16)
        tables.append(jnp.block([[high, low], [high, jnp.zeros_like(low)]]))
    lanes = np.arange(128)
    node = chebyshev_nodes()
    tau = np.zeros((8, 128))
    tau[0], tau[1] = node[(lanes >> 3) & 7], node[lanes & 7]
    vmem = pl.BlockSpec(memory_space=pltpu.VMEM)
    out = pl.pallas_call(
        kernel,
        out_shape=pltpu.VMEM((TILES, 2, 8, 128), F32),
        in_specs=[pl.BlockSpec(memory_space=pltpu.HBM)] * 3,
        out_specs=vmem,
        scratch_shapes=[
            pltpu.VMEM((2, TILES, 4, 2, 128), F32),
            pltpu.VMEM((2, TILES, 8, 128), F32),
            pltpu.VMEM((2, GRID_TILES, 8, 128), F32),
            pltpu.VMEM((2 * LEVELS + 1, TILES, 8, 128), F32),
            pltpu.VMEM((2 * LEVELS + 1, TILES, 8, 128), F32),
            pltpu.VMEM((8, 128), F32),
            pltpu.VMEM((2, 512, 256), BF16),
            pltpu.SemaphoreType.DMA,
            pltpu.SemaphoreType.DMA,
            pltpu.SemaphoreType.DMA,
            pltpu.SemaphoreType.DMA((2,)),
        ],
        compiler_params=pltpu.CompilerParams(collective_id=0, has_side_effects=True),
    )(weights.reshape(256, 2, 128), jnp.asarray(tau, F32), jnp.stack(tables))
    return out.reshape(512, 128)


def solution(mesh):
    spec = P(("outer", "inner"), None)
    return jax.shard_map(body, mesh=mesh, in_specs=(spec,), out_specs=spec, check_vma=False)
```

```python
import functools

import jax
import jax.numpy as jnp
import numpy as np
from jax import lax
from jax.experimental import pallas as pl
from jax.experimental.pallas import tpu as pltpu
from jax.sharding import PartitionSpec as P

LOGICAL = pl.DeviceIdType.LOGICAL
F32 = jnp.float32
BF16 = jnp.bfloat16
GRID_N = 16384.0
LEVELS = 8
TILES = 32
EARLY_PLANES = 2
EXACT = (0, 1, 2, 3, 4, 5, 6, 7)


def chebyshev_nodes():
    return 0.5 * np.cos(np.pi * (2.0 * np.arange(8) + 1.0) / 16.0)


def lagrange_weights(which_child):
    node = chebyshev_nodes()
    targets = (node + which_child - 0.5) / 2.0
    table = np.ones((8, 8))
    for anchor in range(8):
        for other in range(8):
            if other != anchor:
                table[anchor] *= (targets - node[other]) / (node[anchor] - node[other])
    return table


def merge_matrix(dimension):
    parts = []
    for child in range(2):
        table = lagrange_weights(child)
        full = np.kron(table, np.eye(8)) if dimension == 0 else np.kron(np.eye(8), table)
        parts.append(full.T)
    one = np.concatenate(parts, axis=0)
    out = np.zeros((256, 128))
    out[:128, :64] = one
    out[128:, 64:] = one
    return out


def even_fit(values, terms):
    z = 0.125 * (1.0 - np.cos(np.pi * (np.arange(400) + 0.5) / 400))
    basis = np.polynomial.chebyshev.Chebyshev.fit(z, values(np.sqrt(z)), terms - 1, domain=[0, 0.25])
    return [float(c) for c in basis.convert(kind=np.polynomial.Polynomial).coef]


SIN_COEF = even_fit(lambda f: np.sin(2 * np.pi * f) / f, 6)
COS_COEF = even_fit(lambda f: np.cos(2 * np.pi * f), 7)


def horner(coef, z):
    total = jnp.full_like(z, coef[-1])
    for c in coef[-2::-1]:
        total = total * z + c
    return total


def nearest(v):
    return jnp.floor(v + 0.5)


def turn(cycles):
    f = cycles - nearest(cycles)
    z = f * f
    return horner(COS_COEF, z), f * horner(SIN_COEF, z)


def widths(level):
    odd = len([m for m in range(level) if m % 2 == 1])
    even = len([m for m in range(level) if m % 2 == 0])
    h = (2.0 ** -(3 + 4 - odd), 2.0 ** -(4 + 4 - even))
    w = (GRID_N * 2.0 ** -(4 + odd), GRID_N * 2.0 ** -(3 + even))
    return h, w


def place_terms(level):
    terms = []
    for m in range(level, LEVELS):
        e = (m + 1) % 2
        weight = 2.0 ** -(7 - (m - 1) // 2) if e == 0 else 2.0 ** -(8 - m // 2)
        if m == level:
            where = ("lane", 6)
        elif m <= 5:
            where = ("lead", m - 1)
        else:
            where = ("sub", m - 5)
        terms.append((*where, e, weight))
    return terms


def frequency_terms(level):
    terms = [("sub", 0, 0, 1024.0)]
    for m in range(level):
        e = (m + 1) % 2
        weight = 512.0 / 2 ** (m // 2) if e == 0 else 1024.0 / 2 ** (m // 2)
        if m <= 4:
            where = ("lead", m)
        elif m <= 6:
            where = ("sub", m - 4)
        else:
            where = ("lane", 6)
        terms.append((*where, e, weight))
    return terms


def vector_part(terms, e, sub, lane, base):
    total = jnp.full((8, 128), base, F32)
    for where, bit, dim, weight in terms:
        if dim == e and where != "lead":
            source = sub if where == "sub" else lane
            total = total + ((source >> bit) & 1).astype(F32) * weight
    return total


def lead_part(terms, e, index, scale):
    total = jnp.int32(0)
    for where, bit, dim, weight in terms:
        if dim == e and where == "lead":
            total = total + ((index >> bit) & 1) * int(weight * scale)
    return total


def grid_offset(level):
    return sum(max(TILES >> l, 1) for l in range(level))


GRID_TILES = grid_offset(LEVELS + 1)


def device_bits(dest):
    d1 = ((dest >> 6) & 1) + 2 * ((dest >> 7) & 1) + 4 * (dest & 1)
    d2 = (dest >> 1) & 15
    d5 = (dest >> 5) & 1
    return d1, d2, d5


def coefficient_tiles(me, tau_ref, g_ref, sub, lane):
    d1, d2, _ = device_bits(me)
    tau = (tau_ref[0:1, :], tau_ref[1:2, :])
    for level in range(LEVELS + 1):
        h, _ = widths(level)
        terms = place_terms(level)
        base = [vector_part(terms, e, sub, lane, 0.5 * h[e]) + h[e] * tau[e] for e in range(2)]
        count = max(TILES >> level, 1)

        def tile(u, carry, level=level, base=base, terms=terms):
            index = u << level
            x1 = base[0] + (d1 * 32 + lead_part(terms, 0, index, 256)).astype(F32) * (1 / 256)
            x2 = base[1] + (d2 * 16 + lead_part(terms, 1, index, 256)).astype(F32) * (1 / 256)
            cos1, sin1 = turn(x1)
            cos2, sin2 = turn(x2)
            g1 = (2.0 + sin1 * sin2) * (1 / 16)
            g2 = (2.0 + cos1 * cos2) * (1 / 16)
            g_ref[0, grid_offset(level) + u] = g1 * g1
            g_ref[1, grid_offset(level) + u] = g2 * g2
            return carry

        lax.fori_loop(0, count, tile, 0, unroll=min(count, 8))


def factor_tiles(me, level, tau_ref, g_ref, cos_ref, sin_ref, sub, lane):
    _, _, d5 = device_bits(me)
    tau = (tau_ref[0:1, :], tau_ref[1:2, :])
    h, w = widths(level)
    e = (level + 1) % 2
    terms = frequency_terms(level)
    base = [vector_part(terms, d, sub, lane, 0.5 * w[d] - GRID_N / 2) for d in range(2)]
    slope = [h[d] * tau[d] for d in range(2)]

    def whole(k1, k2, g1, g2):
        lin = slope[0] * k1 + slope[1] * k2
        rad = jnp.sqrt(g1 * (k1 * k1) + g2 * (k2 * k2))
        return (lin - nearest(lin)) + (rad - nearest(rad))

    def tile(i, carry):
        k1 = base[0] + lead_part(terms, 0, i, 1).astype(F32)
        k2 = base[1] + (d5 * 2048 + lead_part(terms, 1, i, 1)).astype(F32)
        u = grid_offset(level) + (i >> min(level, 5))
        g1, g2 = g_ref[0, u], g_ref[1, u]
        if level == LEVELS:
            cos_ref[2 * level, i], sin_ref[2 * level, i] = turn(whole(k1, k2, g1, g2))
            return carry
        if level > 0:
            square = g1 * (k1 * k1) + g2 * (k2 * k2)
            rad = jnp.sqrt(square)
        for j in range(2):
            step = (2 * j - 1) * w[e] / 4
            if level == 0:
                cycles = whole(k1, k2 + step, g1, g2)
            else:
                k, g = (k1, g1) if e == 0 else (k2, g2)
                extra = g * (step * (2.0 * k + step))
                cycles = slope[e] * step + extra / (jnp.sqrt(square + extra) + rad)
            cos_ref[2 * level + j, i], sin_ref[2 * level + j, i] = turn(cycles)
        return carry

    lax.fori_loop(0, TILES, tile, 0, unroll=8)


def merge(left, right, w_ref, dimension, exact):
    n = left.shape[0]
    values = [left.reshape(8 * n, 128), right.reshape(8 * n, 128)]
    parts = [v.astype(BF16) for v in values]
    if exact:
        parts += [(v - p.astype(F32)).astype(BF16) for v, p in zip(values, parts)]
    table = w_ref[dimension, : 128 * len(parts)]
    total = jnp.dot(jnp.concatenate(parts, axis=1), table, preferred_element_type=F32)
    return (total[:, :128] + total[:, 128:]).reshape(n, 8, 128)


def load(recv, state, lane):
    low_lane = (lane < 64)[None]
    first, second = recv[0], recv[1]
    state[0] = jnp.where(low_lane, first, pltpu.roll(second, 64, 2))
    state[1] = jnp.where(low_lane, pltpu.roll(first, 64, 2), second)


def run_levels(out_ref, cos_ref, sin_ref, w_ref, state, sub, lane):
    low_lane = lane < 64
    for level in range(LEVELS):
        e = (level + 1) % 2
        exact = level in EXACT
        re, im = state[0], state[1]
        turned = []
        for j in range(2):
            c, s = cos_ref[2 * level + j], sin_ref[2 * level + j]
            turned.append((re * c - im * s, im * c + re * s))
        for part in range(2):
            r0, r1 = turned[0][part], turned[1][part]
            if level < 5:
                lo = 1 << level
                hi = TILES // (2 * lo)
                outs = []
                for r in (r0, r1):
                    v = r.reshape(hi, 2, lo, 8, 128)
                    left = v[:, 0].reshape(16, 8, 128)
                    right = v[:, 1].reshape(16, 8, 128)
                    outs.append(merge(left, right, w_ref, e, exact).reshape(hi, 1, lo, 8, 128))
                new = jnp.concatenate(outs, axis=1).reshape(TILES, 8, 128)
            elif level < 7:
                bit = level - 4
                keep = (((sub >> bit) & 1) == 0)[None]
                shift = 1 << bit
                left = jnp.where(keep, r0, pltpu.roll(r1, shift, 1))
                right = jnp.where(keep, pltpu.roll(r0, 8 - shift, 1), r1)
                new = merge(left, right, w_ref, e, exact)
            else:
                new = merge(r0, r1, w_ref, e, exact)
            state[part] = new
    re, im = state[0], state[1]
    c, s = cos_ref[2 * LEVELS], sin_ref[2 * LEVELS]
    w_re, w_im = re * c + im * s, im * c - re * s
    even = jnp.where(low_lane[None], w_re, pltpu.roll(w_im, 64, 2))
    odd = jnp.where(low_lane[None], pltpu.roll(w_re, 64, 2), w_im)
    out_ref[...] = jnp.concatenate([even[:, None], odd[:, None]], axis=1)


FAR = 0xD0


def kernel(x_ref, tau_hbm, w_hbm, out_ref, recv, state, g_ref, cos_ref, sin_ref, tau_ref, w_ref, send_sem, recv_sem, own_sem, table_sem, ready_sem):
    me = lax.axis_index("outer") * 32 + lax.axis_index("inner")
    barrier = pltpu.get_barrier_semaphore()

    def greet(n, carry):
        pl.semaphore_signal(barrier, inc=1, device_id=me ^ (2 * n ^ FAR), device_id_type=LOGICAL)
        return carry

    lax.fori_loop(0, FAR // 2, greet, 0, unroll=8)
    lax.fori_loop(FAR // 2 + 1, 128, greet, 0, unroll=23)
    pl.semaphore_signal(barrier, inc=1, device_id=me ^ 1, device_id_type=LOGICAL)
    place = recv.at[me & 1, (me >> 1) & 31, me >> 6]
    copies = [
        pltpu.make_async_copy(tau_hbm, tau_ref, table_sem.at[0]),
        pltpu.make_async_copy(w_hbm, w_ref, table_sem.at[1]),
        pltpu.make_async_copy(x_ref.at[(me & 31) * 8 + (me >> 5)], place, own_sem),
    ]
    for copy in copies:
        copy.start()
    sub = lax.broadcasted_iota(jnp.int32, (8, 128), 0)
    lane = lax.broadcasted_iota(jnp.int32, (8, 128), 1)
    copies[0].wait()
    early = ((me >> 2) & 7) < EARLY_PLANES

    def factors():
        coefficient_tiles(me, tau_ref, g_ref, sub, lane)
        for level in range(LEVELS + 1):
            factor_tiles(me, level, tau_ref, g_ref, cos_ref, sin_ref, sub, lane)

    @pl.when(early)
    def _():
        factors()

    pl.semaphore_wait(barrier, 128)
    pl.semaphore_signal(ready_sem, inc=1, device_id=me ^ 1, device_id_type=LOGICAL)

    def send(d):
        pltpu.make_async_remote_copy(
            src_ref=x_ref.at[(d & 31) * 8 + (d >> 5)],
            dst_ref=place,
            send_sem=send_sem,
            recv_sem=recv_sem,
            device_id=d,
            device_id_type=LOGICAL,
        ).start()

    def serve(other):
        base = me ^ FAR ^ other

        def step(n, carry):
            send(base ^ (2 * n))
            return carry

        lax.fori_loop(0, FAR // 2, step, 0, unroll=8)

        @pl.when(other == 1)
        def _():
            send(base ^ FAR)

        lax.fori_loop(FAR // 2 + 1, 128, step, 0, unroll=23)

    core = me & 1

    @pl.when(core == 0)
    def _():
        pl.semaphore_wait(ready_sem, 1)

    serve(1 - core)

    @pl.when(core == 1)
    def _():
        pl.semaphore_wait(ready_sem, 1)

    serve(core)
    for copy in copies[1:]:
        copy.wait()

    @pl.when(jnp.logical_not(early))
    def _():
        factors()

    most = x_ref.at[pl.ds(0, 255)]

    pltpu.make_async_copy(most, most, recv_sem).wait()
    load(recv.reshape(2, TILES, 8, 128), state, lane)
    run_levels(out_ref, cos_ref, sin_ref, w_ref, state, sub, lane)
    pltpu.make_async_copy(most, most, send_sem).wait()


def body(weights):
    tables = []
    for dimension in range(2):
        full = jnp.asarray(merge_matrix(dimension), F32)
        high = full.astype(BF16)
        low = (full - high.astype(F32)).astype(BF16)
        tables.append(jnp.block([[high, low], [high, jnp.zeros_like(low)]]))
    lanes = np.arange(128)
    node = chebyshev_nodes()
    tau = np.zeros((8, 128))
    tau[0], tau[1] = node[(lanes >> 3) & 7], node[lanes & 7]
    vmem = pl.BlockSpec(memory_space=pltpu.VMEM)
    out = pl.pallas_call(
        kernel,
        out_shape=pltpu.VMEM((TILES, 2, 8, 128), F32),
        in_specs=[pl.BlockSpec(memory_space=pltpu.HBM)] * 3,
        out_specs=vmem,
        scratch_shapes=[
            pltpu.VMEM((2, TILES, 4, 2, 128), F32),
            pltpu.VMEM((2, TILES, 8, 128), F32),
            pltpu.VMEM((2, GRID_TILES, 8, 128), F32),
            pltpu.VMEM((2 * LEVELS + 1, TILES, 8, 128), F32),
            pltpu.VMEM((2 * LEVELS + 1, TILES, 8, 128), F32),
            pltpu.VMEM((8, 128), F32),
            pltpu.VMEM((2, 512, 256), BF16),
            pltpu.SemaphoreType.DMA,
            pltpu.SemaphoreType.DMA,
            pltpu.SemaphoreType.DMA,
            pltpu.SemaphoreType.DMA((2,)),
            pltpu.SemaphoreType.REGULAR,
        ],
        compiler_params=pltpu.CompilerParams(collective_id=0, has_side_effects=True),
    )(weights.reshape(256, 2, 128), jnp.asarray(tau, F32), jnp.stack(tables))
    return out.reshape(512, 128)


def solution(mesh):
    spec = P(("outer", "inner"), None)
    return jax.shard_map(body, mesh=mesh, in_specs=(spec,), out_specs=spec, check_vma=False)
```

```python
import functools

import jax
import jax.numpy as jnp
import numpy as np
from jax import lax
from jax.experimental import pallas as pl
from jax.experimental.pallas import tpu as pltpu
from jax.sharding import PartitionSpec as P

LOGICAL = pl.DeviceIdType.LOGICAL
F32 = jnp.float32
BF16 = jnp.bfloat16
GRID_N = 16384.0
LEVELS = 8
TILES = 32
EARLY_PLANES = 2
EXACT = (0, 1, 2, 3, 4, 5, 6, 7)


def chebyshev_nodes():
    return 0.5 * np.cos(np.pi * (2.0 * np.arange(8) + 1.0) / 16.0)


def lagrange_weights(which_child):
    node = chebyshev_nodes()
    targets = (node + which_child - 0.5) / 2.0
    table = np.ones((8, 8))
    for anchor in range(8):
        for other in range(8):
            if other != anchor:
                table[anchor] *= (targets - node[other]) / (node[anchor] - node[other])
    return table


def merge_matrix(dimension):
    parts = []
    for child in range(2):
        table = lagrange_weights(child)
        full = np.kron(table, np.eye(8)) if dimension == 0 else np.kron(np.eye(8), table)
        parts.append(full.T)
    one = np.concatenate(parts, axis=0)
    out = np.zeros((256, 128))
    out[:128, :64] = one
    out[128:, 64:] = one
    return out


def even_fit(values, terms):
    z = 0.125 * (1.0 - np.cos(np.pi * (np.arange(400) + 0.5) / 400))
    basis = np.polynomial.chebyshev.Chebyshev.fit(z, values(np.sqrt(z)), terms - 1, domain=[0, 0.25])
    return [float(c) for c in basis.convert(kind=np.polynomial.Polynomial).coef]


SIN_COEF = even_fit(lambda f: np.sin(2 * np.pi * f) / f, 6)
COS_COEF = even_fit(lambda f: np.cos(2 * np.pi * f), 7)


def horner(coef, z):
    total = jnp.full_like(z, coef[-1])
    for c in coef[-2::-1]:
        total = total * z + c
    return total


def nearest(v):
    return jnp.floor(v + 0.5)


def turn(cycles):
    f = cycles - nearest(cycles)
    z = f * f
    return horner(COS_COEF, z), f * horner(SIN_COEF, z)


def widths(level):
    odd = len([m for m in range(level) if m % 2 == 1])
    even = len([m for m in range(level) if m % 2 == 0])
    h = (2.0 ** -(3 + 4 - odd), 2.0 ** -(4 + 4 - even))
    w = (GRID_N * 2.0 ** -(4 + odd), GRID_N * 2.0 ** -(3 + even))
    return h, w


def place_terms(level):
    terms = []
    for m in range(level, LEVELS):
        e = (m + 1) % 2
        weight = 2.0 ** -(7 - (m - 1) // 2) if e == 0 else 2.0 ** -(8 - m // 2)
        if m == level:
            where = ("lane", 6)
        elif m <= 5:
            where = ("lead", m - 1)
        else:
            where = ("sub", m - 5)
        terms.append((*where, e, weight))
    return terms


def frequency_terms(level):
    terms = [("sub", 0, 0, 1024.0)]
    for m in range(level):
        e = (m + 1) % 2
        weight = 512.0 / 2 ** (m // 2) if e == 0 else 1024.0 / 2 ** (m // 2)
        if m <= 4:
            where = ("lead", m)
        elif m <= 6:
            where = ("sub", m - 4)
        else:
            where = ("lane", 6)
        terms.append((*where, e, weight))
    return terms


def vector_part(terms, e, sub, lane, base):
    total = jnp.full((8, 128), base, F32)
    for where, bit, dim, weight in terms:
        if dim == e and where != "lead":
            source = sub if where == "sub" else lane
            total = total + ((source >> bit) & 1).astype(F32) * weight
    return total


def lead_part(terms, e, index, scale):
    total = jnp.int32(0)
    for where, bit, dim, weight in terms:
        if dim == e and where == "lead":
            total = total + ((index >> bit) & 1) * int(weight * scale)
    return total


def grid_offset(level):
    return sum(max(TILES >> l, 1) for l in range(level))


GRID_TILES = grid_offset(LEVELS + 1)


def device_bits(dest):
    d1 = ((dest >> 6) & 1) + 2 * ((dest >> 7) & 1) + 4 * (dest & 1)
    d2 = (dest >> 1) & 15
    d5 = (dest >> 5) & 1
    return d1, d2, d5


def coefficient_tiles(me, tau_ref, g_ref, sub, lane):
    d1, d2, _ = device_bits(me)
    tau = (tau_ref[0:1, :], tau_ref[1:2, :])
    for level in range(LEVELS + 1):
        h, _ = widths(level)
        terms = place_terms(level)
        base = [vector_part(terms, e, sub, lane, 0.5 * h[e]) + h[e] * tau[e] for e in range(2)]
        count = max(TILES >> level, 1)

        def tile(u, carry, level=level, base=base, terms=terms):
            index = u << level
            x1 = base[0] + (d1 * 32 + lead_part(terms, 0, index, 256)).astype(F32) * (1 / 256)
            x2 = base[1] + (d2 * 16 + lead_part(terms, 1, index, 256)).astype(F32) * (1 / 256)
            cos1, sin1 = turn(x1)
            cos2, sin2 = turn(x2)
            g1 = (2.0 + sin1 * sin2) * (1 / 16)
            g2 = (2.0 + cos1 * cos2) * (1 / 16)
            g_ref[0, grid_offset(level) + u] = g1 * g1
            g_ref[1, grid_offset(level) + u] = g2 * g2
            return carry

        lax.fori_loop(0, count, tile, 0, unroll=min(count, 8))


def factor_tiles(me, level, tau_ref, g_ref, cos_ref, sin_ref, sub, lane):
    _, _, d5 = device_bits(me)
    tau = (tau_ref[0:1, :], tau_ref[1:2, :])
    h, w = widths(level)
    e = (level + 1) % 2
    terms = frequency_terms(level)
    base = [vector_part(terms, d, sub, lane, 0.5 * w[d] - GRID_N / 2) for d in range(2)]
    slope = [h[d] * tau[d] for d in range(2)]

    def whole(k1, k2, g1, g2):
        lin = slope[0] * k1 + slope[1] * k2
        rad = jnp.sqrt(g1 * (k1 * k1) + g2 * (k2 * k2))
        return (lin - nearest(lin)) + (rad - nearest(rad))

    def tile(i, carry):
        k1 = base[0] + lead_part(terms, 0, i, 1).astype(F32)
        k2 = base[1] + (d5 * 2048 + lead_part(terms, 1, i, 1)).astype(F32)
        u = grid_offset(level) + (i >> min(level, 5))
        g1, g2 = g_ref[0, u], g_ref[1, u]
        if level == LEVELS:
            cos_ref[2 * level, i], sin_ref[2 * level, i] = turn(whole(k1, k2, g1, g2))
            return carry
        if level > 0:
            square = g1 * (k1 * k1) + g2 * (k2 * k2)
            rad = jnp.sqrt(square)
        for j in range(2):
            step = (2 * j - 1) * w[e] / 4
            if level == 0:
                cycles = whole(k1, k2 + step, g1, g2)
            else:
                k, g = (k1, g1) if e == 0 else (k2, g2)
                extra = g * (step * (2.0 * k + step))
                cycles = slope[e] * step + extra / (jnp.sqrt(square + extra) + rad)
            cos_ref[2 * level + j, i], sin_ref[2 * level + j, i] = turn(cycles)
        return carry

    lax.fori_loop(0, TILES, tile, 0, unroll=8)


def merge(pairs, w_ref, dimension):
    sides = [jnp.concatenate([pair[i] for pair in pairs], axis=0) for i in range(2)]
    parts = [v.astype(BF16) for v in sides]
    parts += [(v - p.astype(F32)).astype(BF16) for v, p in zip(sides, parts)]
    total = jnp.dot(jnp.concatenate(parts, axis=1), w_ref[dimension], preferred_element_type=F32)
    total = total[:, :128] + total[:, 128:]
    return [total[8 * i : 8 * i + 8] for i in range(len(pairs))]


def chunk_tiles(level, chunk):
    if level < 3 or level > 4:
        return [8 * chunk + i for i in range(8)]
    lows = (2 * chunk, 2 * chunk + 1)
    return [8 * high + low for high in range(4) for low in lows]


def run_chunk(level, tiles, cos_ref, sin_ref, w_ref, state, sub):
    e = (level + 1) % 2
    turned = {}
    for i in tiles:
        re, im = state[0, i], state[1, i]
        for j in range(2):
            c, s = cos_ref[2 * level + j, i], sin_ref[2 * level + j, i]
            turned[i, j] = (re * c - im * s, im * c + re * s)
    pairs, places = [], []
    for i in tiles:
        for part in range(2):
            if level < 5:
                j = (i >> level) & 1
                left = turned[i & ~(1 << level), j][part]
                right = turned[i | 1 << level, j][part]
            else:
                left, right = turned[i, 0][part], turned[i, 1][part]
                if level < 7:
                    keep = ((sub >> (level - 4)) & 1) == 0
                    shift = 1 << (level - 4)
                    left, right = (
                        jnp.where(keep, left, pltpu.roll(right, shift, 0)),
                        jnp.where(keep, pltpu.roll(left, 8 - shift, 0), right),
                    )
            pairs.append((left, right))
            places.append((part, i))
    for (part, i), value in zip(places, merge(pairs, w_ref, e)):
        state[part, i] = value


def load(recv, state, lane):
    low_lane = (lane < 64)[None]
    first, second = recv[0], recv[1]
    state[0] = jnp.where(low_lane, first, pltpu.roll(second, 64, 2))
    state[1] = jnp.where(low_lane, pltpu.roll(first, 64, 2), second)


def run_levels(out_ref, cos_ref, sin_ref, w_ref, state, sub, lane):
    for level in range(LEVELS):
        for chunk in range(4):
            run_chunk(level, chunk_tiles(level, chunk), cos_ref, sin_ref, w_ref, state, sub)
    low_lane = lane < 64
    for i in range(TILES):
        re, im = state[0, i], state[1, i]
        c, s = cos_ref[2 * LEVELS, i], sin_ref[2 * LEVELS, i]
        w_re, w_im = re * c + im * s, im * c - re * s
        out_ref[i, 0] = jnp.where(low_lane, w_re, pltpu.roll(w_im, 64, 1))
        out_ref[i, 1] = jnp.where(low_lane, pltpu.roll(w_re, 64, 1), w_im)


FAR = 0xD0


def kernel(x_ref, tau_hbm, w_hbm, out_ref, recv, state, g_ref, cos_ref, sin_ref, tau_ref, w_ref, send_sem, recv_sem, own_sem, table_sem, ready_sem):
    me = lax.axis_index("outer") * 32 + lax.axis_index("inner")
    barrier = pltpu.get_barrier_semaphore()

    def greet(n, carry):
        pl.semaphore_signal(barrier, inc=1, device_id=me ^ (2 * n ^ FAR), device_id_type=LOGICAL)
        return carry

    lax.fori_loop(0, FAR // 2, greet, 0, unroll=8)
    lax.fori_loop(FAR // 2 + 1, 128, greet, 0, unroll=23)
    pl.semaphore_signal(barrier, inc=1, device_id=me ^ 1, device_id_type=LOGICAL)
    place = recv.at[me & 1, (me >> 1) & 31, me >> 6]
    copies = [
        pltpu.make_async_copy(tau_hbm, tau_ref, table_sem.at[0]),
        pltpu.make_async_copy(w_hbm, w_ref, table_sem.at[1]),
        pltpu.make_async_copy(x_ref.at[(me & 31) * 8 + (me >> 5)], place, own_sem),
    ]
    for copy in copies:
        copy.start()
    sub = lax.broadcasted_iota(jnp.int32, (8, 128), 0)
    lane = lax.broadcasted_iota(jnp.int32, (8, 128), 1)
    copies[0].wait()
    early = ((me >> 2) & 7) < EARLY_PLANES

    def factors():
        coefficient_tiles(me, tau_ref, g_ref, sub, lane)
        for level in range(LEVELS + 1):
            factor_tiles(me, level, tau_ref, g_ref, cos_ref, sin_ref, sub, lane)

    @pl.when(early)
    def _():
        factors()

    pl.semaphore_wait(barrier, 128)
    pl.semaphore_signal(ready_sem, inc=1, device_id=me ^ 1, device_id_type=LOGICAL)

    def send(d):
        pltpu.make_async_remote_copy(
            src_ref=x_ref.at[(d & 31) * 8 + (d >> 5)],
            dst_ref=place,
            send_sem=send_sem,
            recv_sem=recv_sem,
            device_id=d,
            device_id_type=LOGICAL,
        ).start()

    def serve(other):
        base = me ^ FAR ^ other

        def step(n, carry):
            send(base ^ (2 * n))
            return carry

        lax.fori_loop(0, FAR // 2, step, 0, unroll=8)

        @pl.when(other == 1)
        def _():
            send(base ^ FAR)

        lax.fori_loop(FAR // 2 + 1, 128, step, 0, unroll=23)

    core = me & 1

    @pl.when(core == 0)
    def _():
        pl.semaphore_wait(ready_sem, 1)

    serve(1 - core)

    @pl.when(core == 1)
    def _():
        pl.semaphore_wait(ready_sem, 1)

    serve(core)
    for copy in copies[1:]:
        copy.wait()

    @pl.when(jnp.logical_not(early))
    def _():
        factors()

    most = x_ref.at[pl.ds(0, 255)]

    pltpu.make_async_copy(most, most, recv_sem).wait()
    load(recv.reshape(2, TILES, 8, 128), state, lane)
    run_levels(out_ref, cos_ref, sin_ref, w_ref, state, sub, lane)
    pltpu.make_async_copy(most, most, send_sem).wait()


def body(weights):
    tables = []
    for dimension in range(2):
        full = jnp.asarray(merge_matrix(dimension), F32)
        high = full.astype(BF16)
        low = (full - high.astype(F32)).astype(BF16)
        tables.append(jnp.block([[high, low], [high, jnp.zeros_like(low)]]))
    lanes = np.arange(128)
    node = chebyshev_nodes()
    tau = np.zeros((8, 128))
    tau[0], tau[1] = node[(lanes >> 3) & 7], node[lanes & 7]
    vmem = pl.BlockSpec(memory_space=pltpu.VMEM)
    out = pl.pallas_call(
        kernel,
        out_shape=pltpu.VMEM((TILES, 2, 8, 128), F32),
        in_specs=[pl.BlockSpec(memory_space=pltpu.HBM)] * 3,
        out_specs=vmem,
        scratch_shapes=[
            pltpu.VMEM((2, TILES, 4, 2, 128), F32),
            pltpu.VMEM((2, TILES, 8, 128), F32),
            pltpu.VMEM((2, GRID_TILES, 8, 128), F32),
            pltpu.VMEM((2 * LEVELS + 1, TILES, 8, 128), F32),
            pltpu.VMEM((2 * LEVELS + 1, TILES, 8, 128), F32),
            pltpu.VMEM((8, 128), F32),
            pltpu.VMEM((2, 512, 256), BF16),
            pltpu.SemaphoreType.DMA,
            pltpu.SemaphoreType.DMA,
            pltpu.SemaphoreType.DMA,
            pltpu.SemaphoreType.DMA((2,)),
            pltpu.SemaphoreType.REGULAR,
        ],
        compiler_params=pltpu.CompilerParams(collective_id=0, has_side_effects=True),
    )(weights.reshape(256, 2, 128), jnp.asarray(tau, F32), jnp.stack(tables))
    return out.reshape(512, 128)


def solution(mesh):
    spec = P(("outer", "inner"), None)
    return jax.shard_map(body, mesh=mesh, in_specs=(spec,), out_specs=spec, check_vma=False)
```

```python
import functools

import jax
import jax.numpy as jnp
import numpy as np
from jax import lax
from jax.experimental import pallas as pl
from jax.experimental.pallas import tpu as pltpu
from jax.sharding import PartitionSpec as P

LOGICAL = pl.DeviceIdType.LOGICAL
F32 = jnp.float32
BF16 = jnp.bfloat16
GRID_N = 16384.0
LEVELS = 8
TILES = 32
EARLY_PLANES = 3
EXACT = (0, 1, 2, 3, 4, 5, 6, 7)


def chebyshev_nodes():
    return 0.5 * np.cos(np.pi * (2.0 * np.arange(8) + 1.0) / 16.0)


def lagrange_weights(which_child):
    node = chebyshev_nodes()
    targets = (node + which_child - 0.5) / 2.0
    table = np.ones((8, 8))
    for anchor in range(8):
        for other in range(8):
            if other != anchor:
                table[anchor] *= (targets - node[other]) / (node[anchor] - node[other])
    return table


def merge_matrix(dimension):
    parts = []
    for child in range(2):
        table = lagrange_weights(child)
        full = np.kron(table, np.eye(8)) if dimension == 0 else np.kron(np.eye(8), table)
        parts.append(full.T)
    one = np.concatenate(parts, axis=0)
    out = np.zeros((256, 128))
    out[:128, :64] = one
    out[128:, 64:] = one
    return out


def even_fit(values, terms):
    z = 0.125 * (1.0 - np.cos(np.pi * (np.arange(400) + 0.5) / 400))
    basis = np.polynomial.chebyshev.Chebyshev.fit(z, values(np.sqrt(z)), terms - 1, domain=[0, 0.25])
    return [float(c) for c in basis.convert(kind=np.polynomial.Polynomial).coef]


SIN_COEF = even_fit(lambda f: np.sin(2 * np.pi * f) / f, 6)
COS_COEF = even_fit(lambda f: np.cos(2 * np.pi * f), 7)


def horner(coef, z):
    total = jnp.full_like(z, coef[-1])
    for c in coef[-2::-1]:
        total = total * z + c
    return total


def nearest(v):
    return jnp.floor(v + 0.5)


def turn(cycles):
    f = cycles - nearest(cycles)
    z = f * f
    return horner(COS_COEF, z), f * horner(SIN_COEF, z)


def widths(level):
    odd = len([m for m in range(level) if m % 2 == 1])
    even = len([m for m in range(level) if m % 2 == 0])
    h = (2.0 ** -(3 + 4 - odd), 2.0 ** -(4 + 4 - even))
    w = (GRID_N * 2.0 ** -(4 + odd), GRID_N * 2.0 ** -(3 + even))
    return h, w


def place_terms(level):
    terms = []
    for m in range(level, LEVELS):
        e = (m + 1) % 2
        weight = 2.0 ** -(7 - (m - 1) // 2) if e == 0 else 2.0 ** -(8 - m // 2)
        if m == level:
            where = ("lane", 6)
        elif m <= 5:
            where = ("lead", m - 1)
        else:
            where = ("sub", m - 5)
        terms.append((*where, e, weight))
    return terms


def frequency_terms(level):
    terms = [("sub", 0, 0, 1024.0)]
    for m in range(level):
        e = (m + 1) % 2
        weight = 512.0 / 2 ** (m // 2) if e == 0 else 1024.0 / 2 ** (m // 2)
        if m <= 4:
            where = ("lead", m)
        elif m <= 6:
            where = ("sub", m - 4)
        else:
            where = ("lane", 6)
        terms.append((*where, e, weight))
    return terms


def vector_part(terms, e, sub, lane, base):
    total = jnp.full((8, 128), base, F32)
    for where, bit, dim, weight in terms:
        if dim == e and where != "lead":
            source = sub if where == "sub" else lane
            total = total + ((source >> bit) & 1).astype(F32) * weight
    return total


def lead_part(terms, e, index, scale):
    total = jnp.int32(0)
    for where, bit, dim, weight in terms:
        if dim == e and where == "lead":
            total = total + ((index >> bit) & 1) * int(weight * scale)
    return total


def grid_offset(level):
    return sum(max(TILES >> l, 1) for l in range(level))


GRID_TILES = grid_offset(LEVELS + 1)


def device_bits(dest):
    d1 = ((dest >> 6) & 1) + 2 * ((dest >> 7) & 1) + 4 * (dest & 1)
    d2 = (dest >> 1) & 15
    d5 = (dest >> 5) & 1
    return d1, d2, d5


def coefficient_tiles(me, tau_ref, g_ref, sub, lane):
    d1, d2, _ = device_bits(me)
    tau = (tau_ref[0:1, :], tau_ref[1:2, :])
    for level in range(LEVELS + 1):
        h, _ = widths(level)
        terms = place_terms(level)
        base = [vector_part(terms, e, sub, lane, 0.5 * h[e]) + h[e] * tau[e] for e in range(2)]
        count = max(TILES >> level, 1)

        def tile(u, carry, level=level, base=base, terms=terms):
            index = u << level
            x1 = base[0] + (d1 * 32 + lead_part(terms, 0, index, 256)).astype(F32) * (1 / 256)
            x2 = base[1] + (d2 * 16 + lead_part(terms, 1, index, 256)).astype(F32) * (1 / 256)
            cos1, sin1 = turn(x1)
            cos2, sin2 = turn(x2)
            g1 = (2.0 + sin1 * sin2) * (1 / 16)
            g2 = (2.0 + cos1 * cos2) * (1 / 16)
            g_ref[0, grid_offset(level) + u] = g1 * g1
            g_ref[1, grid_offset(level) + u] = g2 * g2
            return carry

        lax.fori_loop(0, count, tile, 0, unroll=min(count, 8))


def factor_tiles(me, level, tau_ref, g_ref, cos_ref, sin_ref, sub, lane):
    _, _, d5 = device_bits(me)
    tau = (tau_ref[0:1, :], tau_ref[1:2, :])
    h, w = widths(level)
    e = (level + 1) % 2
    terms = frequency_terms(level)
    base = [vector_part(terms, d, sub, lane, 0.5 * w[d] - GRID_N / 2) for d in range(2)]
    slope = [h[d] * tau[d] for d in range(2)]

    def whole(k1, k2, g1, g2):
        lin = slope[0] * k1 + slope[1] * k2
        rad = jnp.sqrt(g1 * (k1 * k1) + g2 * (k2 * k2))
        return (lin - nearest(lin)) + (rad - nearest(rad))

    def tile(i, carry):
        k1 = base[0] + lead_part(terms, 0, i, 1).astype(F32)
        k2 = base[1] + (d5 * 2048 + lead_part(terms, 1, i, 1)).astype(F32)
        u = grid_offset(level) + (i >> min(level, 5))
        g1, g2 = g_ref[0, u], g_ref[1, u]
        if level == LEVELS:
            cos_ref[2 * level, i], sin_ref[2 * level, i] = turn(whole(k1, k2, g1, g2))
            return carry
        if level > 0:
            square = g1 * (k1 * k1) + g2 * (k2 * k2)
            rad = jnp.sqrt(square)
        for j in range(2):
            step = (2 * j - 1) * w[e] / 4
            if level == 0:
                cycles = whole(k1, k2 + step, g1, g2)
            else:
                k, g = (k1, g1) if e == 0 else (k2, g2)
                extra = g * (step * (2.0 * k + step))
                cycles = slope[e] * step + extra / (jnp.sqrt(square + extra) + rad)
            cos_ref[2 * level + j, i], sin_ref[2 * level + j, i] = turn(cycles)
        return carry

    lax.fori_loop(0, TILES, tile, 0, unroll=8)


def merge(pairs, w_ref, dimension):
    sides = [jnp.concatenate([pair[i] for pair in pairs], axis=0) for i in range(2)]
    parts = [v.astype(BF16) for v in sides]
    parts += [(v - p.astype(F32)).astype(BF16) for v, p in zip(sides, parts)]
    total = jnp.dot(jnp.concatenate(parts, axis=1), w_ref[dimension], preferred_element_type=F32)
    total = total[:, :128] + total[:, 128:]
    return [total[8 * i : 8 * i + 8] for i in range(len(pairs))]


def chunk_tiles(level, chunk):
    if level < 3 or level > 4:
        return [8 * chunk + i for i in range(8)]
    lows = (2 * chunk, 2 * chunk + 1)
    return [8 * high + low for high in range(4) for low in lows]


def run_chunk(level, tiles, cos_ref, sin_ref, w_ref, state, sub):
    e = (level + 1) % 2
    turned = {}
    for i in tiles:
        re, im = state[0, i], state[1, i]
        for j in range(2):
            c, s = cos_ref[2 * level + j, i], sin_ref[2 * level + j, i]
            turned[i, j] = (re * c - im * s, im * c + re * s)
    pairs, places = [], []
    for i in tiles:
        for part in range(2):
            if level < 5:
                j = (i >> level) & 1
                left = turned[i & ~(1 << level), j][part]
                right = turned[i | 1 << level, j][part]
            else:
                left, right = turned[i, 0][part], turned[i, 1][part]
                if level < 7:
                    keep = ((sub >> (level - 4)) & 1) == 0
                    shift = 1 << (level - 4)
                    left, right = (
                        jnp.where(keep, left, pltpu.roll(right, shift, 0)),
                        jnp.where(keep, pltpu.roll(left, 8 - shift, 0), right),
                    )
            pairs.append((left, right))
            places.append((part, i))
    for (part, i), value in zip(places, merge(pairs, w_ref, e)):
        state[part, i] = value


def load(recv, state, lane):
    low_lane = (lane < 64)[None]
    first, second = recv[0], recv[1]
    state[0] = jnp.where(low_lane, first, pltpu.roll(second, 64, 2))
    state[1] = jnp.where(low_lane, pltpu.roll(first, 64, 2), second)


def run_levels(out_ref, cos_ref, sin_ref, w_ref, state, sub, lane):
    for level in range(LEVELS):
        for chunk in range(4):
            run_chunk(level, chunk_tiles(level, chunk), cos_ref, sin_ref, w_ref, state, sub)
    low_lane = lane < 64
    for i in range(TILES):
        re, im = state[0, i], state[1, i]
        c, s = cos_ref[2 * LEVELS, i], sin_ref[2 * LEVELS, i]
        w_re, w_im = re * c + im * s, im * c - re * s
        out_ref[i, 0] = jnp.where(low_lane, w_re, pltpu.roll(w_im, 64, 1))
        out_ref[i, 1] = jnp.where(low_lane, pltpu.roll(w_re, 64, 1), w_im)


FAR = 0xD0


def kernel(x_ref, tau_hbm, w_hbm, out_ref, recv, state, g_ref, cos_ref, sin_ref, tau_ref, w_ref, held, send_sem, recv_sem, own_sem, table_sem, ready_sem, held_sem):
    me = lax.axis_index("outer") * 32 + lax.axis_index("inner")
    barrier = pltpu.get_barrier_semaphore()
    hold = pltpu.make_async_copy(x_ref, held, held_sem)
    hold.start()

    def greet(n, carry):
        pl.semaphore_signal(barrier, inc=1, device_id=me ^ (2 * n ^ FAR), device_id_type=LOGICAL)
        return carry

    lax.fori_loop(0, FAR // 2, greet, 0, unroll=8)
    lax.fori_loop(FAR // 2 + 1, 128, greet, 0, unroll=23)
    pl.semaphore_signal(barrier, inc=1, device_id=me ^ 1, device_id_type=LOGICAL)
    place = recv.at[me & 1, (me >> 1) & 31, me >> 6]
    copies = [
        pltpu.make_async_copy(tau_hbm, tau_ref, table_sem.at[0]),
        pltpu.make_async_copy(w_hbm, w_ref, table_sem.at[1]),
        pltpu.make_async_copy(x_ref.at[(me & 31) * 8 + (me >> 5)], place, own_sem),
    ]
    for copy in copies:
        copy.start()
    sub = lax.broadcasted_iota(jnp.int32, (8, 128), 0)
    lane = lax.broadcasted_iota(jnp.int32, (8, 128), 1)
    copies[0].wait()
    early = ((me >> 2) & 7) < EARLY_PLANES

    def factors():
        coefficient_tiles(me, tau_ref, g_ref, sub, lane)
        for level in range(LEVELS + 1):
            factor_tiles(me, level, tau_ref, g_ref, cos_ref, sin_ref, sub, lane)

    @pl.when(early)
    def _():
        factors()

    hold.wait()
    pl.semaphore_wait(barrier, 128)
    pl.semaphore_signal(ready_sem, inc=1, device_id=me ^ 1, device_id_type=LOGICAL)

    def send(d):
        pltpu.make_async_remote_copy(
            src_ref=held.at[(d & 31) * 8 + (d >> 5)],
            dst_ref=place,
            send_sem=send_sem,
            recv_sem=recv_sem,
            device_id=d,
            device_id_type=LOGICAL,
        ).start()

    def serve(other):
        base = me ^ FAR ^ other

        def step(n, carry):
            send(base ^ (2 * n))
            return carry

        lax.fori_loop(0, FAR // 2, step, 0, unroll=8)

        @pl.when(other == 1)
        def _():
            send(base ^ FAR)

        lax.fori_loop(FAR // 2 + 1, 128, step, 0, unroll=23)

    core = me & 1

    @pl.when(core == 0)
    def _():
        pl.semaphore_wait(ready_sem, 1)

    serve(1 - core)

    @pl.when(core == 1)
    def _():
        pl.semaphore_wait(ready_sem, 1)

    serve(core)
    for copy in copies[1:]:
        copy.wait()

    @pl.when(jnp.logical_not(early))
    def _():
        factors()

    most = x_ref.at[pl.ds(0, 255)]

    pltpu.make_async_copy(most, most, recv_sem).wait()
    load(recv.reshape(2, TILES, 8, 128), state, lane)
    run_levels(out_ref, cos_ref, sin_ref, w_ref, state, sub, lane)
    pltpu.make_async_copy(most, most, send_sem).wait()


def body(weights):
    tables = []
    for dimension in range(2):
        full = jnp.asarray(merge_matrix(dimension), F32)
        high = full.astype(BF16)
        low = (full - high.astype(F32)).astype(BF16)
        tables.append(jnp.block([[high, low], [high, jnp.zeros_like(low)]]))
    lanes = np.arange(128)
    node = chebyshev_nodes()
    tau = np.zeros((8, 128))
    tau[0], tau[1] = node[(lanes >> 3) & 7], node[lanes & 7]
    vmem = pl.BlockSpec(memory_space=pltpu.VMEM)
    out = pl.pallas_call(
        kernel,
        out_shape=pltpu.VMEM((TILES, 2, 8, 128), F32),
        in_specs=[pl.BlockSpec(memory_space=pltpu.HBM)] * 3,
        out_specs=vmem,
        scratch_shapes=[
            pltpu.VMEM((2, TILES, 4, 2, 128), F32),
            pltpu.VMEM((2, TILES, 8, 128), F32),
            pltpu.VMEM((2, GRID_TILES, 8, 128), F32),
            pltpu.VMEM((2 * LEVELS + 1, TILES, 8, 128), F32),
            pltpu.VMEM((2 * LEVELS + 1, TILES, 8, 128), F32),
            pltpu.VMEM((8, 128), F32),
            pltpu.VMEM((2, 512, 256), BF16),
            pltpu.VMEM((256, 2, 128), F32),
            pltpu.SemaphoreType.DMA,
            pltpu.SemaphoreType.DMA,
            pltpu.SemaphoreType.DMA,
            pltpu.SemaphoreType.DMA((2,)),
            pltpu.SemaphoreType.REGULAR,
            pltpu.SemaphoreType.DMA,
        ],
        compiler_params=pltpu.CompilerParams(collective_id=0, has_side_effects=True),
    )(weights.reshape(256, 2, 128), jnp.asarray(tau, F32), jnp.stack(tables))
    return out.reshape(512, 128)


def solution(mesh):
    spec = P(("outer", "inner"), None)
    return jax.shard_map(body, mesh=mesh, in_specs=(spec,), out_specs=spec, check_vma=False)
```

```python
import functools

import jax
import jax.numpy as jnp
import numpy as np
from jax import lax
from jax.experimental import pallas as pl
from jax.experimental.pallas import tpu as pltpu
from jax.sharding import PartitionSpec as P

LOGICAL = pl.DeviceIdType.LOGICAL
F32 = jnp.float32
BF16 = jnp.bfloat16
GRID_N = 16384.0
LEVELS = 8
TILES = 32
EARLY_PLANES = 3
EXACT = (0, 1, 2, 3, 4, 5, 6, 7)


def chebyshev_nodes():
    return 0.5 * np.cos(np.pi * (2.0 * np.arange(8) + 1.0) / 16.0)


def lagrange_weights(which_child):
    node = chebyshev_nodes()
    targets = (node + which_child - 0.5) / 2.0
    table = np.ones((8, 8))
    for anchor in range(8):
        for other in range(8):
            if other != anchor:
                table[anchor] *= (targets - node[other]) / (node[anchor] - node[other])
    return table


def merge_matrix(dimension):
    parts = []
    for child in range(2):
        table = lagrange_weights(child)
        full = np.kron(table, np.eye(8)) if dimension == 0 else np.kron(np.eye(8), table)
        parts.append(full.T)
    one = np.concatenate(parts, axis=0)
    out = np.zeros((256, 128))
    out[:128, :64] = one
    out[128:, 64:] = one
    return out


def even_fit(values, terms):
    z = 0.125 * (1.0 - np.cos(np.pi * (np.arange(400) + 0.5) / 400))
    basis = np.polynomial.chebyshev.Chebyshev.fit(z, values(np.sqrt(z)), terms - 1, domain=[0, 0.25])
    return [float(c) for c in basis.convert(kind=np.polynomial.Polynomial).coef]


SIN_COEF = even_fit(lambda f: np.sin(2 * np.pi * f) / f, 6)
COS_COEF = even_fit(lambda f: np.cos(2 * np.pi * f), 7)


def horner(coef, z):
    total = jnp.full_like(z, coef[-1])
    for c in coef[-2::-1]:
        total = total * z + c
    return total


def nearest(v):
    return jnp.floor(v + 0.5)


def turn(cycles):
    f = cycles - nearest(cycles)
    z = f * f
    return horner(COS_COEF, z), f * horner(SIN_COEF, z)


def widths(level):
    odd = len([m for m in range(level) if m % 2 == 1])
    even = len([m for m in range(level) if m % 2 == 0])
    h = (2.0 ** -(3 + 4 - odd), 2.0 ** -(4 + 4 - even))
    w = (GRID_N * 2.0 ** -(4 + odd), GRID_N * 2.0 ** -(3 + even))
    return h, w


def place_terms(level):
    terms = []
    for m in range(level, LEVELS):
        e = (m + 1) % 2
        weight = 2.0 ** -(7 - (m - 1) // 2) if e == 0 else 2.0 ** -(8 - m // 2)
        if m == level:
            where = ("lane", 6)
        elif m <= 5:
            where = ("lead", m - 1)
        else:
            where = ("sub", m - 5)
        terms.append((*where, e, weight))
    return terms


def frequency_terms(level):
    terms = [("sub", 0, 0, 1024.0)]
    for m in range(level):
        e = (m + 1) % 2
        weight = 512.0 / 2 ** (m // 2) if e == 0 else 1024.0 / 2 ** (m // 2)
        if m <= 4:
            where = ("lead", m)
        elif m <= 6:
            where = ("sub", m - 4)
        else:
            where = ("lane", 6)
        terms.append((*where, e, weight))
    return terms


def vector_part(terms, e, sub, lane, base):
    total = jnp.full((8, 128), base, F32)
    for where, bit, dim, weight in terms:
        if dim == e and where != "lead":
            source = sub if where == "sub" else lane
            total = total + ((source >> bit) & 1).astype(F32) * weight
    return total


def lead_part(terms, e, index, scale):
    total = jnp.int32(0)
    for where, bit, dim, weight in terms:
        if dim == e and where == "lead":
            total = total + ((index >> bit) & 1) * int(weight * scale)
    return total


def grid_offset(level):
    return sum(max(TILES >> l, 1) for l in range(level))


GRID_TILES = grid_offset(LEVELS + 1)


def device_bits(dest):
    d1 = ((dest >> 6) & 1) + 2 * ((dest >> 7) & 1) + 4 * (dest & 1)
    d2 = (dest >> 1) & 15
    d5 = (dest >> 5) & 1
    return d1, d2, d5


def coefficient_tiles(me, tau_ref, g_ref, sub, lane):
    d1, d2, _ = device_bits(me)
    tau = (tau_ref[0:1, :], tau_ref[1:2, :])
    for level in range(LEVELS + 1):
        h, _ = widths(level)
        terms = place_terms(level)
        base = [vector_part(terms, e, sub, lane, 0.5 * h[e]) + h[e] * tau[e] for e in range(2)]
        count = max(TILES >> level, 1)

        def tile(u, carry, level=level, base=base, terms=terms):
            index = u << level
            x1 = base[0] + (d1 * 32 + lead_part(terms, 0, index, 256)).astype(F32) * (1 / 256)
            x2 = base[1] + (d2 * 16 + lead_part(terms, 1, index, 256)).astype(F32) * (1 / 256)
            cos1, sin1 = turn(x1)
            cos2, sin2 = turn(x2)
            g1 = (2.0 + sin1 * sin2) * (1 / 16)
            g2 = (2.0 + cos1 * cos2) * (1 / 16)
            g_ref[0, grid_offset(level) + u] = g1 * g1
            g_ref[1, grid_offset(level) + u] = g2 * g2
            return carry

        lax.fori_loop(0, count, tile, 0, unroll=min(count, 8))


def factor_tiles(me, level, tau_ref, g_ref, cos_ref, sin_ref, sub, lane):
    _, _, d5 = device_bits(me)
    tau = (tau_ref[0:1, :], tau_ref[1:2, :])
    h, w = widths(level)
    e = (level + 1) % 2
    terms = frequency_terms(level)
    base = [vector_part(terms, d, sub, lane, 0.5 * w[d] - GRID_N / 2) for d in range(2)]
    slope = [h[d] * tau[d] for d in range(2)]

    def whole(k1, k2, g1, g2):
        lin = slope[0] * k1 + slope[1] * k2
        rad = jnp.sqrt(g1 * (k1 * k1) + g2 * (k2 * k2))
        return (lin - nearest(lin)) + (rad - nearest(rad))

    def tile(i, carry):
        k1 = base[0] + lead_part(terms, 0, i, 1).astype(F32)
        k2 = base[1] + (d5 * 2048 + lead_part(terms, 1, i, 1)).astype(F32)
        u = grid_offset(level) + (i >> min(level, 5))
        g1, g2 = g_ref[0, u], g_ref[1, u]
        if level == LEVELS:
            cos_ref[2 * level, i], sin_ref[2 * level, i] = turn(whole(k1, k2, g1, g2))
            return carry
        if level > 0:
            square = g1 * (k1 * k1) + g2 * (k2 * k2)
            rad = jnp.sqrt(square)
        for j in range(2):
            step = (2 * j - 1) * w[e] / 4
            if level == 0:
                cycles = whole(k1, k2 + step, g1, g2)
            else:
                k, g = (k1, g1) if e == 0 else (k2, g2)
                extra = g * (step * (2.0 * k + step))
                cycles = slope[e] * step + extra / (jnp.sqrt(square + extra) + rad)
            cos_ref[2 * level + j, i], sin_ref[2 * level + j, i] = turn(cycles)
        return carry

    lax.fori_loop(0, TILES, tile, 0, unroll=8)


def merge(pairs, w_ref, dimension):
    sides = [jnp.concatenate([pair[i] for pair in pairs], axis=0) for i in range(2)]
    parts = [v.astype(BF16) for v in sides]
    parts += [(v - p.astype(F32)).astype(BF16) for v, p in zip(sides, parts)]
    total = jnp.dot(jnp.concatenate(parts, axis=1), w_ref[dimension], preferred_element_type=F32)
    total = total[:, :128] + total[:, 128:]
    return [total[8 * i : 8 * i + 8] for i in range(len(pairs))]


def chunk_tiles(level, chunk):
    if level < 3 or level > 4:
        return [8 * chunk + i for i in range(8)]
    lows = (2 * chunk, 2 * chunk + 1)
    return [8 * high + low for high in range(4) for low in lows]


def run_chunk(level, tiles, cos_ref, sin_ref, w_ref, state, sub):
    e = (level + 1) % 2
    turned = {}
    for i in tiles:
        re, im = state[0, i], state[1, i]
        for j in range(2):
            c, s = cos_ref[2 * level + j, i], sin_ref[2 * level + j, i]
            turned[i, j] = (re * c - im * s, im * c + re * s)
    pairs, places = [], []
    for i in tiles:
        for part in range(2):
            if level < 5:
                j = (i >> level) & 1
                left = turned[i & ~(1 << level), j][part]
                right = turned[i | 1 << level, j][part]
            else:
                left, right = turned[i, 0][part], turned[i, 1][part]
                if level < 7:
                    keep = ((sub >> (level - 4)) & 1) == 0
                    shift = 1 << (level - 4)
                    left, right = (
                        jnp.where(keep, left, pltpu.roll(right, shift, 0)),
                        jnp.where(keep, pltpu.roll(left, 8 - shift, 0), right),
                    )
            pairs.append((left, right))
            places.append((part, i))
    for (part, i), value in zip(places, merge(pairs, w_ref, e)):
        state[part, i] = value


def load(recv, state, lane):
    low_lane = (lane < 64)[None]
    first, second = recv[0], recv[1]
    state[0] = jnp.where(low_lane, first, pltpu.roll(second, 64, 2))
    state[1] = jnp.where(low_lane, pltpu.roll(first, 64, 2), second)


def run_levels(out_ref, cos_ref, sin_ref, w_ref, state, sub, lane):
    for level in range(LEVELS):
        for chunk in range(4):
            run_chunk(level, chunk_tiles(level, chunk), cos_ref, sin_ref, w_ref, state, sub)
    low_lane = lane < 64
    for i in range(TILES):
        re, im = state[0, i], state[1, i]
        c, s = cos_ref[2 * LEVELS, i], sin_ref[2 * LEVELS, i]
        w_re, w_im = re * c + im * s, im * c - re * s
        out_ref[i, 0] = jnp.where(low_lane, w_re, pltpu.roll(w_im, 64, 1))
        out_ref[i, 1] = jnp.where(low_lane, pltpu.roll(w_re, 64, 1), w_im)


FAR = 0xD0


def kernel(x_ref, tau_hbm, w_hbm, out_ref, recv, state, g_ref, cos_ref, sin_ref, tau_ref, w_ref, held, send_sem, recv_sem, own_sem, table_sem, ready_sem, held_sem):
    me = lax.axis_index("outer") * 32 + lax.axis_index("inner")
    barrier = pltpu.get_barrier_semaphore()
    hold = pltpu.make_async_copy(x_ref, held, held_sem)
    hold.start()

    def greet(n, carry):
        pl.semaphore_signal(barrier, inc=1, device_id=me ^ (2 * n ^ FAR), device_id_type=LOGICAL)
        return carry

    lax.fori_loop(0, FAR // 2, greet, 0, unroll=8)
    lax.fori_loop(FAR // 2 + 1, 128, greet, 0, unroll=23)
    pl.semaphore_signal(barrier, inc=1, device_id=me ^ 1, device_id_type=LOGICAL)
    place = recv.at[me & 1, (me >> 1) & 31, me >> 6]
    copies = [
        pltpu.make_async_copy(tau_hbm, tau_ref, table_sem.at[0]),
        pltpu.make_async_copy(w_hbm, w_ref, table_sem.at[1]),
        pltpu.make_async_copy(x_ref.at[(me & 31) * 8 + (me >> 5)], place, own_sem),
    ]
    for copy in copies:
        copy.start()
    sub = lax.broadcasted_iota(jnp.int32, (8, 128), 0)
    lane = lax.broadcasted_iota(jnp.int32, (8, 128), 1)
    copies[0].wait()
    early = ((me >> 2) & 7) < EARLY_PLANES

    def factors():
        coefficient_tiles(me, tau_ref, g_ref, sub, lane)
        for level in range(LEVELS + 1):
            factor_tiles(me, level, tau_ref, g_ref, cos_ref, sin_ref, sub, lane)

    @pl.when(early)
    def _():
        factors()

    hold.wait()
    pl.semaphore_wait(barrier, 128)
    pl.semaphore_signal(ready_sem, inc=1, device_id=me ^ 1, device_id_type=LOGICAL)

    def send(d):
        pltpu.make_async_remote_copy(
            src_ref=held.at[(d & 31) * 8 + (d >> 5)],
            dst_ref=place,
            send_sem=send_sem,
            recv_sem=recv_sem,
            device_id=d,
            device_id_type=LOGICAL,
        ).start()

    def serve(core, half):
        base = ((me ^ FAR) & ~17) | core | 16 * half

        def step(n, carry):
            for m in range(8):
                send(base ^ (32 * n) ^ (2 * m))
            return carry

        lax.fori_loop(0, FAR >> 5, step, 0)

        @pl.when((base ^ (FAR & 0xE0)) != me)
        def _():
            send(base ^ (FAR & 0xE0))

        for m in range(1, 8):
            send(base ^ (FAR & 0xE0) ^ (2 * m))
        lax.fori_loop((FAR >> 5) + 1, 8, step, 0)

    @pl.when(me & 1 == 0)
    def _():
        pl.semaphore_wait(ready_sem, 1)

    serve(1, 0)
    @pl.when(me & 1 == 1)
    def _():
        pl.semaphore_wait(ready_sem, 1)

    serve(0, 0)
    serve(1, 1)
    serve(0, 1)
    for copy in copies[1:]:
        copy.wait()

    @pl.when(jnp.logical_not(early))
    def _():
        factors()

    most = x_ref.at[pl.ds(0, 255)]

    pltpu.make_async_copy(most, most, recv_sem).wait()
    load(recv.reshape(2, TILES, 8, 128), state, lane)
    run_levels(out_ref, cos_ref, sin_ref, w_ref, state, sub, lane)
    pltpu.make_async_copy(most, most, send_sem).wait()


def body(weights):
    tables = []
    for dimension in range(2):
        full = jnp.asarray(merge_matrix(dimension), F32)
        high = full.astype(BF16)
        low = (full - high.astype(F32)).astype(BF16)
        tables.append(jnp.block([[high, low], [high, jnp.zeros_like(low)]]))
    lanes = np.arange(128)
    node = chebyshev_nodes()
    tau = np.zeros((8, 128))
    tau[0], tau[1] = node[(lanes >> 3) & 7], node[lanes & 7]
    vmem = pl.BlockSpec(memory_space=pltpu.VMEM)
    out = pl.pallas_call(
        kernel,
        out_shape=pltpu.VMEM((TILES, 2, 8, 128), F32),
        in_specs=[pl.BlockSpec(memory_space=pltpu.HBM)] * 3,
        out_specs=vmem,
        scratch_shapes=[
            pltpu.VMEM((2, TILES, 4, 2, 128), F32),
            pltpu.VMEM((2, TILES, 8, 128), F32),
            pltpu.VMEM((2, GRID_TILES, 8, 128), F32),
            pltpu.VMEM((2 * LEVELS + 1, TILES, 8, 128), F32),
            pltpu.VMEM((2 * LEVELS + 1, TILES, 8, 128), F32),
            pltpu.VMEM((8, 128), F32),
            pltpu.VMEM((2, 512, 256), BF16),
            pltpu.VMEM((256, 2, 128), F32),
            pltpu.SemaphoreType.DMA,
            pltpu.SemaphoreType.DMA,
            pltpu.SemaphoreType.DMA,
            pltpu.SemaphoreType.DMA((2,)),
            pltpu.SemaphoreType.REGULAR,
            pltpu.SemaphoreType.DMA,
        ],
        compiler_params=pltpu.CompilerParams(collective_id=0, has_side_effects=True),
    )(weights.reshape(256, 2, 128), jnp.asarray(tau, F32), jnp.stack(tables))
    return out.reshape(512, 128)


def solution(mesh):
    spec = P(("outer", "inner"), None)
    return jax.shard_map(body, mesh=mesh, in_specs=(spec,), out_specs=spec, check_vma=False)
```

```python
import functools

import jax
import jax.numpy as jnp
import numpy as np
from jax import lax
from jax.experimental import pallas as pl
from jax.experimental.pallas import tpu as pltpu
from jax.sharding import PartitionSpec as P

LOGICAL = pl.DeviceIdType.LOGICAL
F32 = jnp.float32
BF16 = jnp.bfloat16
GRID_N = 16384.0
LEVELS = 8
TILES = 32
EARLY_PLANES = 3
EXACT = (0, 1, 2, 3, 4, 5, 6, 7)


def chebyshev_nodes():
    return 0.5 * np.cos(np.pi * (2.0 * np.arange(8) + 1.0) / 16.0)


def lagrange_weights(which_child):
    node = chebyshev_nodes()
    targets = (node + which_child - 0.5) / 2.0
    table = np.ones((8, 8))
    for anchor in range(8):
        for other in range(8):
            if other != anchor:
                table[anchor] *= (targets - node[other]) / (node[anchor] - node[other])
    return table


def merge_matrix(dimension):
    parts = []
    for child in range(2):
        table = lagrange_weights(child)
        full = np.kron(table, np.eye(8)) if dimension == 0 else np.kron(np.eye(8), table)
        parts.append(full.T)
    one = np.concatenate(parts, axis=0)
    out = np.zeros((256, 128))
    out[:128, :64] = one
    out[128:, 64:] = one
    return out


def even_fit(values, terms):
    z = 0.125 * (1.0 - np.cos(np.pi * (np.arange(400) + 0.5) / 400))
    basis = np.polynomial.chebyshev.Chebyshev.fit(z, values(np.sqrt(z)), terms - 1, domain=[0, 0.25])
    return [float(c) for c in basis.convert(kind=np.polynomial.Polynomial).coef]


SIN_COEF = even_fit(lambda f: np.sin(2 * np.pi * f) / f, 6)
COS_COEF = even_fit(lambda f: np.cos(2 * np.pi * f), 7)


def horner(coef, z):
    total = jnp.full_like(z, coef[-1])
    for c in coef[-2::-1]:
        total = total * z + c
    return total


def nearest(v):
    return jnp.floor(v + 0.5)


def turn(cycles):
    f = cycles - nearest(cycles)
    z = f * f
    return horner(COS_COEF, z), f * horner(SIN_COEF, z)


def widths(level):
    odd = len([m for m in range(level) if m % 2 == 1])
    even = len([m for m in range(level) if m % 2 == 0])
    h = (2.0 ** -(3 + 4 - odd), 2.0 ** -(4 + 4 - even))
    w = (GRID_N * 2.0 ** -(4 + odd), GRID_N * 2.0 ** -(3 + even))
    return h, w


def place_terms(level):
    terms = []
    for m in range(level, LEVELS):
        e = (m + 1) % 2
        weight = 2.0 ** -(7 - (m - 1) // 2) if e == 0 else 2.0 ** -(8 - m // 2)
        if m == level:
            where = ("lane", 6)
        elif m <= 5:
            where = ("lead", m - 1)
        else:
            where = ("sub", m - 5)
        terms.append((*where, e, weight))
    return terms


def frequency_terms(level):
    terms = [("sub", 0, 0, 1024.0)]
    for m in range(level):
        e = (m + 1) % 2
        weight = 512.0 / 2 ** (m // 2) if e == 0 else 1024.0 / 2 ** (m // 2)
        if m <= 4:
            where = ("lead", m)
        elif m <= 6:
            where = ("sub", m - 4)
        else:
            where = ("lane", 6)
        terms.append((*where, e, weight))
    return terms


def vector_part(terms, e, sub, lane, base):
    total = jnp.full((8, 128), base, F32)
    for where, bit, dim, weight in terms:
        if dim == e and where != "lead":
            source = sub if where == "sub" else lane
            total = total + ((source >> bit) & 1).astype(F32) * weight
    return total


def lead_part(terms, e, index, scale):
    total = jnp.int32(0)
    for where, bit, dim, weight in terms:
        if dim == e and where == "lead":
            total = total + ((index >> bit) & 1) * int(weight * scale)
    return total


def grid_offset(level):
    return sum(max(TILES >> l, 1) for l in range(level))


GRID_TILES = grid_offset(LEVELS + 1)


def device_bits(dest):
    d1 = ((dest >> 6) & 1) + 2 * ((dest >> 7) & 1) + 4 * (dest & 1)
    d2 = (dest >> 1) & 15
    d5 = (dest >> 5) & 1
    return d1, d2, d5


def coefficient_tiles(me, tau_ref, g_ref, sub, lane):
    d1, d2, _ = device_bits(me)
    tau = (tau_ref[0:1, :], tau_ref[1:2, :])
    for level in range(LEVELS + 1):
        h, _ = widths(level)
        terms = place_terms(level)
        base = [vector_part(terms, e, sub, lane, 0.5 * h[e]) + h[e] * tau[e] for e in range(2)]
        count = max(TILES >> level, 1)

        def tile(u, carry, level=level, base=base, terms=terms):
            index = u << level
            x1 = base[0] + (d1 * 32 + lead_part(terms, 0, index, 256)).astype(F32) * (1 / 256)
            x2 = base[1] + (d2 * 16 + lead_part(terms, 1, index, 256)).astype(F32) * (1 / 256)
            cos1, sin1 = turn(x1)
            cos2, sin2 = turn(x2)
            g1 = (2.0 + sin1 * sin2) * (1 / 16)
            g2 = (2.0 + cos1 * cos2) * (1 / 16)
            g_ref[0, grid_offset(level) + u] = g1 * g1
            g_ref[1, grid_offset(level) + u] = g2 * g2
            return carry

        lax.fori_loop(0, count, tile, 0, unroll=min(count, 8))


def factor_tiles(me, level, tau_ref, g_ref, cos_ref, sin_ref, sub, lane):
    _, _, d5 = device_bits(me)
    tau = (tau_ref[0:1, :], tau_ref[1:2, :])
    h, w = widths(level)
    e = (level + 1) % 2
    terms = frequency_terms(level)
    base = [vector_part(terms, d, sub, lane, 0.5 * w[d] - GRID_N / 2) for d in range(2)]
    slope = [h[d] * tau[d] for d in range(2)]

    def whole(k1, k2, g1, g2):
        lin = slope[0] * k1 + slope[1] * k2
        rad = jnp.sqrt(g1 * (k1 * k1) + g2 * (k2 * k2))
        return (lin - nearest(lin)) + (rad - nearest(rad))

    def tile(i, carry):
        k1 = base[0] + lead_part(terms, 0, i, 1).astype(F32)
        k2 = base[1] + (d5 * 2048 + lead_part(terms, 1, i, 1)).astype(F32)
        u = grid_offset(level) + (i >> min(level, 5))
        g1, g2 = g_ref[0, u], g_ref[1, u]
        if level == LEVELS:
            cos_ref[2 * level, i], sin_ref[2 * level, i] = turn(whole(k1, k2, g1, g2))
            return carry
        if level > 0:
            square = g1 * (k1 * k1) + g2 * (k2 * k2)
            rad = jnp.sqrt(square)
        for j in range(2):
            step = (2 * j - 1) * w[e] / 4
            if level == 0:
                cycles = whole(k1, k2 + step, g1, g2)
            else:
                k, g = (k1, g1) if e == 0 else (k2, g2)
                extra = g * (step * (2.0 * k + step))
                cycles = slope[e] * step + extra / (jnp.sqrt(square + extra) + rad)
            cos_ref[2 * level + j, i], sin_ref[2 * level + j, i] = turn(cycles)
        return carry

    lax.fori_loop(0, TILES, tile, 0, unroll=8)


def merge(pairs, w_ref, dimension):
    sides = [jnp.concatenate([pair[i] for pair in pairs], axis=0) for i in range(2)]
    parts = [v.astype(BF16) for v in sides]
    parts += [(v - p.astype(F32)).astype(BF16) for v, p in zip(sides, parts)]
    total = jnp.dot(jnp.concatenate(parts, axis=1), w_ref[dimension], preferred_element_type=F32)
    total = total[:, :128] + total[:, 128:]
    return [total[8 * i : 8 * i + 8] for i in range(len(pairs))]


def chunk_tiles(level, chunk):
    if level < 3 or level > 4:
        return [8 * chunk + i for i in range(8)]
    lows = (2 * chunk, 2 * chunk + 1)
    return [8 * high + low for high in range(4) for low in lows]


def run_chunk(level, tiles, cos_ref, sin_ref, w_ref, state, sub):
    e = (level + 1) % 2
    turned = {}
    for i in tiles:
        re, im = state[0, i], state[1, i]
        for j in range(2):
            c, s = cos_ref[2 * level + j, i], sin_ref[2 * level + j, i]
            turned[i, j] = (re * c - im * s, im * c + re * s)
    pairs, places = [], []
    for i in tiles:
        for part in range(2):
            if level < 5:
                j = (i >> level) & 1
                left = turned[i & ~(1 << level), j][part]
                right = turned[i | 1 << level, j][part]
            else:
                left, right = turned[i, 0][part], turned[i, 1][part]
                if level < 7:
                    keep = ((sub >> (level - 4)) & 1) == 0
                    shift = 1 << (level - 4)
                    left, right = (
                        jnp.where(keep, left, pltpu.roll(right, shift, 0)),
                        jnp.where(keep, pltpu.roll(left, 8 - shift, 0), right),
                    )
            pairs.append((left, right))
            places.append((part, i))
    for (part, i), value in zip(places, merge(pairs, w_ref, e)):
        state[part, i] = value


def load(recv, state, lane):
    low_lane = (lane < 64)[None]
    first, second = recv[0], recv[1]
    state[0] = jnp.where(low_lane, first, pltpu.roll(second, 64, 2))
    state[1] = jnp.where(low_lane, pltpu.roll(first, 64, 2), second)


def run_levels(out_ref, cos_ref, sin_ref, w_ref, state, sub, lane):
    for level in range(LEVELS):
        for chunk in range(4):
            run_chunk(level, chunk_tiles(level, chunk), cos_ref, sin_ref, w_ref, state, sub)
    low_lane = lane < 64
    for i in range(TILES):
        re, im = state[0, i], state[1, i]
        c, s = cos_ref[2 * LEVELS, i], sin_ref[2 * LEVELS, i]
        w_re, w_im = re * c + im * s, im * c - re * s
        out_ref[i, 0] = jnp.where(low_lane, w_re, pltpu.roll(w_im, 64, 1))
        out_ref[i, 1] = jnp.where(low_lane, pltpu.roll(w_re, 64, 1), w_im)


FAR = 0xD0


def kernel(x_ref, tau_hbm, w_hbm, out_ref, recv, state, g_ref, cos_ref, sin_ref, tau_ref, w_ref, held, send_sem, recv_sem, own_sem, table_sem, ready_sem, held_sem):
    me = lax.axis_index("outer") * 32 + lax.axis_index("inner")
    barrier = pltpu.get_barrier_semaphore()
    hold = pltpu.make_async_copy(x_ref, held, held_sem)
    hold.start()

    def greet(n, carry):
        pl.semaphore_signal(barrier, inc=1, device_id=me ^ (2 * n ^ FAR), device_id_type=LOGICAL)
        return carry

    lax.fori_loop(0, FAR // 2, greet, 0, unroll=8)
    lax.fori_loop(FAR // 2 + 1, 128, greet, 0, unroll=23)
    pl.semaphore_signal(barrier, inc=1, device_id=me ^ 1, device_id_type=LOGICAL)
    place = recv.at[me & 1, (me >> 1) & 31, me >> 6]
    copies = [
        pltpu.make_async_copy(tau_hbm, tau_ref, table_sem.at[0]),
        pltpu.make_async_copy(w_hbm, w_ref, table_sem.at[1]),
        pltpu.make_async_copy(x_ref.at[(me & 31) * 8 + (me >> 5)], place, own_sem),
    ]
    for copy in copies:
        copy.start()
    sub = lax.broadcasted_iota(jnp.int32, (8, 128), 0)
    lane = lax.broadcasted_iota(jnp.int32, (8, 128), 1)
    copies[0].wait()
    early = ((me >> 2) & 7) < EARLY_PLANES

    def factors():
        coefficient_tiles(me, tau_ref, g_ref, sub, lane)
        for level in range(LEVELS + 1):
            factor_tiles(me, level, tau_ref, g_ref, cos_ref, sin_ref, sub, lane)

    @pl.when(early)
    def _():
        factors()

    hold.wait()
    pl.semaphore_wait(barrier, 128)
    pl.semaphore_signal(ready_sem, inc=1, device_id=me ^ 1, device_id_type=LOGICAL)

    def send(d):
        pltpu.make_async_remote_copy(
            src_ref=held.at[(d & 31) * 8 + (d >> 5)],
            dst_ref=place,
            send_sem=send_sem,
            recv_sem=recv_sem,
            device_id=d,
            device_id_type=LOGICAL,
        ).start()

    def serve(core, half):
        base = ((me ^ FAR) & ~17) | core | 16 * half

        def step(n, carry):
            for m in range(8):
                send(base ^ (32 * n) ^ (2 * m))
            return carry

        lax.fori_loop(0, FAR >> 5, step, 0, unroll=True)

        @pl.when((base ^ (FAR & 0xE0)) != me)
        def _():
            send(base ^ (FAR & 0xE0))

        for m in range(1, 8):
            send(base ^ (FAR & 0xE0) ^ (2 * m))
        lax.fori_loop((FAR >> 5) + 1, 8, step, 0, unroll=True)

    @pl.when(me & 1 == 0)
    def _():
        pl.semaphore_wait(ready_sem, 1)

    serve(1, 0)
    @pl.when(me & 1 == 1)
    def _():
        pl.semaphore_wait(ready_sem, 1)

    serve(0, 0)
    serve(1, 1)
    serve(0, 1)
    for copy in copies[1:]:
        copy.wait()

    @pl.when(jnp.logical_not(early))
    def _():
        factors()

    most = x_ref.at[pl.ds(0, 255)]

    pltpu.make_async_copy(most, most, recv_sem).wait()
    load(recv.reshape(2, TILES, 8, 128), state, lane)
    run_levels(out_ref, cos_ref, sin_ref, w_ref, state, sub, lane)
    pltpu.make_async_copy(most, most, send_sem).wait()


def body(weights):
    tables = []
    for dimension in range(2):
        full = jnp.asarray(merge_matrix(dimension), F32)
        high = full.astype(BF16)
        low = (full - high.astype(F32)).astype(BF16)
        tables.append(jnp.block([[high, low], [high, jnp.zeros_like(low)]]))
    lanes = np.arange(128)
    node = chebyshev_nodes()
    tau = np.zeros((8, 128))
    tau[0], tau[1] = node[(lanes >> 3) & 7], node[lanes & 7]
    vmem = pl.BlockSpec(memory_space=pltpu.VMEM)
    out = pl.pallas_call(
        kernel,
        out_shape=pltpu.VMEM((TILES, 2, 8, 128), F32),
        in_specs=[pl.BlockSpec(memory_space=pltpu.HBM)] * 3,
        out_specs=vmem,
        scratch_shapes=[
            pltpu.VMEM((2, TILES, 4, 2, 128), F32),
            pltpu.VMEM((2, TILES, 8, 128), F32),
            pltpu.VMEM((2, GRID_TILES, 8, 128), F32),
            pltpu.VMEM((2 * LEVELS + 1, TILES, 8, 128), F32),
            pltpu.VMEM((2 * LEVELS + 1, TILES, 8, 128), F32),
            pltpu.VMEM((8, 128), F32),
            pltpu.VMEM((2, 512, 256), BF16),
            pltpu.VMEM((256, 2, 128), F32),
            pltpu.SemaphoreType.DMA,
            pltpu.SemaphoreType.DMA,
            pltpu.SemaphoreType.DMA,
            pltpu.SemaphoreType.DMA((2,)),
            pltpu.SemaphoreType.REGULAR,
            pltpu.SemaphoreType.DMA,
        ],
        compiler_params=pltpu.CompilerParams(collective_id=0, has_side_effects=True),
    )(weights.reshape(256, 2, 128), jnp.asarray(tau, F32), jnp.stack(tables))
    return out.reshape(512, 128)


def solution(mesh):
    spec = P(("outer", "inner"), None)
    return jax.shard_map(body, mesh=mesh, in_specs=(spec,), out_specs=spec, check_vma=False)
```

```python
import functools

import jax
import jax.numpy as jnp
import numpy as np
from jax import lax
from jax.experimental import pallas as pl
from jax.experimental.pallas import tpu as pltpu
from jax.sharding import PartitionSpec as P

LOGICAL = pl.DeviceIdType.LOGICAL
F32 = jnp.float32
BF16 = jnp.bfloat16
GRID_N = 16384.0
LEVELS = 8
TILES = 32
EARLY_PLANES = 3
EXACT = (0, 1, 2, 3, 4, 5, 6, 7)


def chebyshev_nodes():
    return 0.5 * np.cos(np.pi * (2.0 * np.arange(8) + 1.0) / 16.0)


def lagrange_weights(which_child):
    node = chebyshev_nodes()
    targets = (node + which_child - 0.5) / 2.0
    table = np.ones((8, 8))
    for anchor in range(8):
        for other in range(8):
            if other != anchor:
                table[anchor] *= (targets - node[other]) / (node[anchor] - node[other])
    return table


def merge_matrix(dimension):
    parts = []
    for child in range(2):
        table = lagrange_weights(child)
        full = np.kron(table, np.eye(8)) if dimension == 0 else np.kron(np.eye(8), table)
        parts.append(full.T)
    one = np.concatenate(parts, axis=0)
    out = np.zeros((256, 128))
    out[:128, :64] = one
    out[128:, 64:] = one
    return out


def even_fit(values, terms):
    z = 0.125 * (1.0 - np.cos(np.pi * (np.arange(400) + 0.5) / 400))
    basis = np.polynomial.chebyshev.Chebyshev.fit(z, values(np.sqrt(z)), terms - 1, domain=[0, 0.25])
    return [float(c) for c in basis.convert(kind=np.polynomial.Polynomial).coef]


SIN_COEF = even_fit(lambda f: np.sin(2 * np.pi * f) / f, 6)
COS_COEF = even_fit(lambda f: np.cos(2 * np.pi * f), 7)


def horner(coef, z):
    total = jnp.full_like(z, coef[-1])
    for c in coef[-2::-1]:
        total = total * z + c
    return total


def nearest(v):
    return jnp.floor(v + 0.5)


def turn(cycles):
    f = cycles - nearest(cycles)
    z = f * f
    return horner(COS_COEF, z), f * horner(SIN_COEF, z)


def widths(level):
    odd = len([m for m in range(level) if m % 2 == 1])
    even = len([m for m in range(level) if m % 2 == 0])
    h = (2.0 ** -(3 + 4 - odd), 2.0 ** -(4 + 4 - even))
    w = (GRID_N * 2.0 ** -(4 + odd), GRID_N * 2.0 ** -(3 + even))
    return h, w


def place_terms(level):
    terms = []
    for m in range(level, LEVELS):
        e = (m + 1) % 2
        weight = 2.0 ** -(7 - (m - 1) // 2) if e == 0 else 2.0 ** -(8 - m // 2)
        if m == level:
            where = ("lane", 6)
        elif m <= 5:
            where = ("lead", m - 1)
        else:
            where = ("sub", m - 5)
        terms.append((*where, e, weight))
    return terms


def frequency_terms(level):
    terms = [("sub", 0, 0, 1024.0)]
    for m in range(level):
        e = (m + 1) % 2
        weight = 512.0 / 2 ** (m // 2) if e == 0 else 1024.0 / 2 ** (m // 2)
        if m <= 4:
            where = ("lead", m)
        elif m <= 6:
            where = ("sub", m - 4)
        else:
            where = ("lane", 6)
        terms.append((*where, e, weight))
    return terms


def vector_part(terms, e, sub, lane, base):
    total = jnp.full((8, 128), base, F32)
    for where, bit, dim, weight in terms:
        if dim == e and where != "lead":
            source = sub if where == "sub" else lane
            total = total + ((source >> bit) & 1).astype(F32) * weight
    return total


def lead_part(terms, e, index, scale):
    total = jnp.int32(0)
    for where, bit, dim, weight in terms:
        if dim == e and where == "lead":
            total = total + ((index >> bit) & 1) * int(weight * scale)
    return total


def grid_offset(level):
    return sum(max(TILES >> l, 1) for l in range(level))


GRID_TILES = grid_offset(LEVELS + 1)


def device_bits(dest):
    d1 = ((dest >> 6) & 1) + 2 * ((dest >> 7) & 1) + 4 * (dest & 1)
    d2 = (dest >> 1) & 15
    d5 = (dest >> 5) & 1
    return d1, d2, d5


def coefficient_tiles(me, tau_ref, g_ref, sub, lane):
    d1, d2, _ = device_bits(me)
    tau = (tau_ref[0:1, :], tau_ref[1:2, :])
    for level in range(LEVELS + 1):
        h, _ = widths(level)
        terms = place_terms(level)
        base = [vector_part(terms, e, sub, lane, 0.5 * h[e]) + h[e] * tau[e] for e in range(2)]
        count = max(TILES >> level, 1)

        def tile(u, carry, level=level, base=base, terms=terms):
            index = u << level
            x1 = base[0] + (d1 * 32 + lead_part(terms, 0, index, 256)).astype(F32) * (1 / 256)
            x2 = base[1] + (d2 * 16 + lead_part(terms, 1, index, 256)).astype(F32) * (1 / 256)
            cos1, sin1 = turn(x1)
            cos2, sin2 = turn(x2)
            g1 = (2.0 + sin1 * sin2) * (1 / 16)
            g2 = (2.0 + cos1 * cos2) * (1 / 16)
            g_ref[0, grid_offset(level) + u] = g1 * g1
            g_ref[1, grid_offset(level) + u] = g2 * g2
            return carry

        lax.fori_loop(0, count, tile, 0, unroll=min(count, 8))


def factor_tiles(me, level, tau_ref, g_ref, cos_ref, sin_ref, sub, lane):
    _, _, d5 = device_bits(me)
    tau = (tau_ref[0:1, :], tau_ref[1:2, :])
    h, w = widths(level)
    e = (level + 1) % 2
    terms = frequency_terms(level)
    base = [vector_part(terms, d, sub, lane, 0.5 * w[d] - GRID_N / 2) for d in range(2)]
    slope = [h[d] * tau[d] for d in range(2)]

    def whole(k1, k2, g1, g2):
        lin = slope[0] * k1 + slope[1] * k2
        rad = jnp.sqrt(g1 * (k1 * k1) + g2 * (k2 * k2))
        return (lin - nearest(lin)) + (rad - nearest(rad))

    def tile(i, carry):
        k1 = base[0] + lead_part(terms, 0, i, 1).astype(F32)
        k2 = base[1] + (d5 * 2048 + lead_part(terms, 1, i, 1)).astype(F32)
        u = grid_offset(level) + (i >> min(level, 5))
        g1, g2 = g_ref[0, u], g_ref[1, u]
        if level == LEVELS:
            cos_ref[2 * level, i], sin_ref[2 * level, i] = turn(whole(k1, k2, g1, g2))
            return carry
        if level > 0:
            square = g1 * (k1 * k1) + g2 * (k2 * k2)
            rad = jnp.sqrt(square)
        for j in range(2):
            step = (2 * j - 1) * w[e] / 4
            if level == 0:
                cycles = whole(k1, k2 + step, g1, g2)
            else:
                k, g = (k1, g1) if e == 0 else (k2, g2)
                extra = g * (step * (2.0 * k + step))
                cycles = slope[e] * step + extra / (jnp.sqrt(square + extra) + rad)
            cos_ref[2 * level + j, i], sin_ref[2 * level + j, i] = turn(cycles)
        return carry

    lax.fori_loop(0, TILES, tile, 0, unroll=8)


def merge(pairs, w_ref, dimension):
    sides = [jnp.concatenate([pair[i] for pair in pairs], axis=0) for i in range(2)]
    parts = [v.astype(BF16) for v in sides]
    parts += [(v - p.astype(F32)).astype(BF16) for v, p in zip(sides, parts)]
    total = jnp.dot(jnp.concatenate(parts, axis=1), w_ref[dimension], preferred_element_type=F32)
    total = total[:, :128] + total[:, 128:]
    return [total[8 * i : 8 * i + 8] for i in range(len(pairs))]


def chunk_tiles(level, chunk):
    if level < 3 or level > 4:
        return [8 * chunk + i for i in range(8)]
    lows = (2 * chunk, 2 * chunk + 1)
    return [8 * high + low for high in range(4) for low in lows]


def run_chunk(level, tiles, cos_ref, sin_ref, w_ref, state, sub):
    e = (level + 1) % 2
    turned = {}
    for i in tiles:
        re, im = state[0, i], state[1, i]
        for j in range(2):
            c, s = cos_ref[2 * level + j, i], sin_ref[2 * level + j, i]
            turned[i, j] = (re * c - im * s, im * c + re * s)
    pairs, places = [], []
    for i in tiles:
        for part in range(2):
            if level < 5:
                j = (i >> level) & 1
                left = turned[i & ~(1 << level), j][part]
                right = turned[i | 1 << level, j][part]
            else:
                left, right = turned[i, 0][part], turned[i, 1][part]
                if level < 7:
                    keep = ((sub >> (level - 4)) & 1) == 0
                    shift = 1 << (level - 4)
                    left, right = (
                        jnp.where(keep, left, pltpu.roll(right, shift, 0)),
                        jnp.where(keep, pltpu.roll(left, 8 - shift, 0), right),
                    )
            pairs.append((left, right))
            places.append((part, i))
    for (part, i), value in zip(places, merge(pairs, w_ref, e)):
        state[part, i] = value


def load(recv, state, lane):
    low_lane = (lane < 64)[None]
    first, second = recv[0], recv[1]
    state[0] = jnp.where(low_lane, first, pltpu.roll(second, 64, 2))
    state[1] = jnp.where(low_lane, pltpu.roll(first, 64, 2), second)


def run_levels(out_ref, cos_ref, sin_ref, w_ref, state, sub, lane):
    for level in range(LEVELS):
        for chunk in range(4):
            run_chunk(level, chunk_tiles(level, chunk), cos_ref, sin_ref, w_ref, state, sub)
    low_lane = lane < 64
    for i in range(TILES):
        re, im = state[0, i], state[1, i]
        c, s = cos_ref[2 * LEVELS, i], sin_ref[2 * LEVELS, i]
        w_re, w_im = re * c + im * s, im * c - re * s
        out_ref[i, 0] = jnp.where(low_lane, w_re, pltpu.roll(w_im, 64, 1))
        out_ref[i, 1] = jnp.where(low_lane, pltpu.roll(w_re, 64, 1), w_im)


FAR = 0xD0


def kernel(x_ref, tau_hbm, w_hbm, out_ref, recv, state, g_ref, cos_ref, sin_ref, tau_ref, w_ref, held, send_sem, recv_sem, own_sem, table_sem, ready_sem, held_sem):
    me = lax.axis_index("outer") * 32 + lax.axis_index("inner")
    barrier = pltpu.get_barrier_semaphore()
    hold = pltpu.make_async_copy(x_ref, held, held_sem)
    hold.start()

    def greet(n, carry):
        pl.semaphore_signal(barrier, inc=1, device_id=me ^ (2 * n ^ FAR), device_id_type=LOGICAL)
        return carry

    lax.fori_loop(0, FAR // 2, greet, 0, unroll=True)
    lax.fori_loop(FAR // 2 + 1, 128, greet, 0, unroll=23)
    pl.semaphore_signal(barrier, inc=1, device_id=me ^ 1, device_id_type=LOGICAL)
    place = recv.at[me & 1, (me >> 1) & 31, me >> 6]
    copies = [
        pltpu.make_async_copy(tau_hbm, tau_ref, table_sem.at[0]),
        pltpu.make_async_copy(w_hbm, w_ref, table_sem.at[1]),
        pltpu.make_async_copy(x_ref.at[(me & 31) * 8 + (me >> 5)], place, own_sem),
    ]
    for copy in copies:
        copy.start()
    sub = lax.broadcasted_iota(jnp.int32, (8, 128), 0)
    lane = lax.broadcasted_iota(jnp.int32, (8, 128), 1)
    copies[0].wait()
    early = ((me >> 2) & 7) < EARLY_PLANES

    def factors():
        coefficient_tiles(me, tau_ref, g_ref, sub, lane)
        for level in range(LEVELS + 1):
            factor_tiles(me, level, tau_ref, g_ref, cos_ref, sin_ref, sub, lane)

    @pl.when(early)
    def _():
        factors()

    hold.wait()
    pl.semaphore_wait(barrier, 128)
    pl.semaphore_signal(ready_sem, inc=1, device_id=me ^ 1, device_id_type=LOGICAL)

    def send(d):
        pltpu.make_async_remote_copy(
            src_ref=held.at[(d & 31) * 8 + (d >> 5)],
            dst_ref=place,
            send_sem=send_sem,
            recv_sem=recv_sem,
            device_id=d,
            device_id_type=LOGICAL,
        ).start()

    def serve(core, half):
        base = ((me ^ FAR) & ~17) | core | 16 * half

        def step(n, carry):
            for m in range(8):
                send(base ^ (32 * n) ^ (2 * m))
            return carry

        lax.fori_loop(0, FAR >> 5, step, 0, unroll=True)

        @pl.when((base ^ (FAR & 0xE0)) != me)
        def _():
            send(base ^ (FAR & 0xE0))

        for m in range(1, 8):
            send(base ^ (FAR & 0xE0) ^ (2 * m))
        lax.fori_loop((FAR >> 5) + 1, 8, step, 0, unroll=True)

    @pl.when(me & 1 == 0)
    def _():
        pl.semaphore_wait(ready_sem, 1)

    serve(1, 0)
    @pl.when(me & 1 == 1)
    def _():
        pl.semaphore_wait(ready_sem, 1)

    serve(0, 0)
    serve(1, 1)
    serve(0, 1)
    for copy in copies[1:]:
        copy.wait()

    @pl.when(jnp.logical_not(early))
    def _():
        factors()

    most = x_ref.at[pl.ds(0, 255)]

    pltpu.make_async_copy(most, most, recv_sem).wait()
    load(recv.reshape(2, TILES, 8, 128), state, lane)
    run_levels(out_ref, cos_ref, sin_ref, w_ref, state, sub, lane)
    pltpu.make_async_copy(most, most, send_sem).wait()


def body(weights):
    tables = []
    for dimension in range(2):
        full = jnp.asarray(merge_matrix(dimension), F32)
        high = full.astype(BF16)
        low = (full - high.astype(F32)).astype(BF16)
        tables.append(jnp.block([[high, low], [high, jnp.zeros_like(low)]]))
    lanes = np.arange(128)
    node = chebyshev_nodes()
    tau = np.zeros((8, 128))
    tau[0], tau[1] = node[(lanes >> 3) & 7], node[lanes & 7]
    vmem = pl.BlockSpec(memory_space=pltpu.VMEM)
    out = pl.pallas_call(
        kernel,
        out_shape=pltpu.VMEM((TILES, 2, 8, 128), F32),
        in_specs=[pl.BlockSpec(memory_space=pltpu.HBM)] * 3,
        out_specs=vmem,
        scratch_shapes=[
            pltpu.VMEM((2, TILES, 4, 2, 128), F32),
            pltpu.VMEM((2, TILES, 8, 128), F32),
            pltpu.VMEM((2, GRID_TILES, 8, 128), F32),
            pltpu.VMEM((2 * LEVELS + 1, TILES, 8, 128), F32),
            pltpu.VMEM((2 * LEVELS + 1, TILES, 8, 128), F32),
            pltpu.VMEM((8, 128), F32),
            pltpu.VMEM((2, 512, 256), BF16),
            pltpu.VMEM((256, 2, 128), F32),
            pltpu.SemaphoreType.DMA,
            pltpu.SemaphoreType.DMA,
            pltpu.SemaphoreType.DMA,
            pltpu.SemaphoreType.DMA((2,)),
            pltpu.SemaphoreType.REGULAR,
            pltpu.SemaphoreType.DMA,
        ],
        compiler_params=pltpu.CompilerParams(collective_id=0, has_side_effects=True),
    )(weights.reshape(256, 2, 128), jnp.asarray(tau, F32), jnp.stack(tables))
    return out.reshape(512, 128)


def solution(mesh):
    spec = P(("outer", "inner"), None)
    return jax.shard_map(body, mesh=mesh, in_specs=(spec,), out_specs=spec, check_vma=False)
```
